32 devices in a mesh: dp: 4 (over y, x), ctx: 8 (over z, core).
Axes of the slice: x: 2, y: 2, z: 4, core: 2. Of those that a mesh axis runs over, the one named last changes fastest.
Arguments:
- signal: bfloat16 [4, 1024, 2048], P('dp', 'ctx'), may hold values from -6 to 6
- gate_input: bfloat16 [4, 1024, 2048], P('dp', 'ctx'), may hold values from -6 to 6
- cotangent: bfloat16 [4, 1024, 2048], P('dp', 'ctx'), may hold values from -6 to 6
- long_filter: float32 [128, 1024], P('ctx'), may hold values from -0.1875 to 0.1875
- short_taps: bfloat16 [128, 2048], replicated, may hold values from -0.5 to 0.5
- skip_gain: float32 [2048], P('ctx'), may hold values from -4 to 4
Outputs:
- output: bfloat16 [4, 1024, 2048], P('dp', 'ctx')
- gate_grad: bfloat16 [4, 1024, 2048], P('dp', 'ctx')
- signal_grad: bfloat16 [4, 1024, 2048], P('dp', 'ctx')
- long_grad: float32 [128, 1024], P('ctx')
- taps_grad: float32 [128, 2048], P(None, 'ctx')
- skip_grad: float32 [2048], P('ctx')
The draws below stay inside these ranges and needn't reach their ends.
All inputs are finite; a program needn't handle non-finite values.
Results may differ from the reference program's by a relative error of at most 0.0058.
Values may be sent and summed in bfloat16 or wider, within the bound.
No kernel may reach another device: no remote copies, remote signals or barrier semaphores. Data moves between devices by JAX's collectives and lax.ppermute only.
A program may use at most 64 MiB of HBM per device.

```python
import math
import jax
import jax.numpy as jnp
from jax import lax

D = 2048
TAPS = 128
L = 1024
G = 128
NB = 4


def shard_levels(stream_key, shape, shards, low, top_value):
    factor_of = 1.0
    for axis_at, blocks in shards:
        steps = jax.random.uniform(jax.random.fold_in(jax.random.fold_in(stream_key, 6), axis_at), (blocks,), jnp.float32, low / len(shards), top_value / len(shards))
        factor_of = factor_of * jnp.repeat(jnp.exp(steps), shape[axis_at] // blocks).reshape((-1,) + (1,) * (len(shape) - 1 - axis_at))
    return factor_of


def bell_draw(rng, dims, spread, reach, split=(), held_as=jnp.bfloat16):
    loudness = shard_levels(rng, dims, split, -0.22, 0.18) if split else 1.0
    result = jax.random.normal(rng, dims, jnp.float32) * spread * loudness
    return jnp.minimum(jnp.maximum(result, -reach), reach).astype(held_as)


def setup_inputs(seed: int = 0) -> dict:
    key_list = jax.random.split(jax.random.key(seed), 7)
    return {
        "signal": bell_draw(key_list[0], (NB, L, D), 1.0, 6.0, ((0, 4), (1, 8))),
        "gate_input": bell_draw(key_list[1], (NB, L, D), 1.0, 6.0, ((0, 4), (1, 8))),
        "cotangent": bell_draw(key_list[2], (NB, L, D), 1.0, 6.0, ((0, 4), (1, 8))),
        "long_filter": bell_draw(key_list[3], (G, L), L ** -0.5, 0.1875, ((0, 8),), jnp.float32),
        "short_taps": bell_draw(key_list[4], (TAPS, D), TAPS ** -0.5, 0.5),
        "skip_gain": bell_draw(key_list[5], (D,), 1.0, 4.0, ((0, 8),), jnp.float32),
    }


def spectrum(values, size):
    return jnp.fft.rfft(values, size, axis=-1)

def back_to_time(spec, size, keep):
    return jnp.fft.irfft(spec, size, axis=-1)[..., :keep]

def reference(signal, gate_input, cotangent, long_filter, short_taps, skip_gain):
    seq_count, seq_length, chan_count = signal.shape
    tap_count = short_taps.shape[0]
    group_count = long_filter.shape[0]
    group_size = chan_count // group_count
    size = 2 * seq_length
    filter_spec = spectrum(jnp.repeat(long_filter.astype(jnp.float32), group_size, axis=0), size)
    taps_spec = spectrum(short_taps.astype(jnp.float32).T, size)
    gains = skip_gain.astype(jnp.float32)[:, None]

    def one_sequence(carry, item):
        series, gating, upstream = item
        series_t = series.astype(jnp.float32).T
        series_spec = spectrum(series_t, size)
        mixed = back_to_time(series_spec * taps_spec, size, seq_length).astype(jnp.bfloat16)
        mixed_f = lax.optimization_barrier(mixed).astype(jnp.float32)
        grad_gate = (upstream.astype(jnp.float32) * gating.astype(jnp.float32)).astype(jnp.bfloat16)
        grad_f = lax.optimization_barrier(grad_gate).astype(jnp.float32).T
        mixed_spec = spectrum(mixed_f, size)
        grad_spec = spectrum(grad_f, size)
        conv = (back_to_time(mixed_spec * filter_spec, size, seq_length) + gains * mixed_f).astype(jnp.bfloat16)
        conv_f = lax.optimization_barrier(conv).astype(jnp.float32).T
        output = (gating.astype(jnp.float32) * conv_f).astype(jnp.bfloat16)
        gate_grad = (upstream.astype(jnp.float32) * conv_f).astype(jnp.bfloat16)
        back_sig = (back_to_time(grad_spec * jnp.conj(filter_spec), size, seq_length) + gains * grad_f).astype(jnp.bfloat16)
        back_f = lax.optimization_barrier(back_sig).astype(jnp.float32)
        back_spec = spectrum(back_f, size)
        signal_grad = back_to_time(back_spec * jnp.conj(taps_spec), size, seq_length).astype(jnp.bfloat16).T
        taps_part = back_to_time(back_spec * jnp.conj(series_spec), size, tap_count)
        long_part = back_to_time(grad_spec * jnp.conj(mixed_spec), size, seq_length)
        long_part = lax.optimization_barrier(jnp.sum(long_part.reshape(group_count, group_size, seq_length), axis=1))
        skip_part = lax.optimization_barrier(jnp.sum(grad_f * mixed_f, axis=1))
        carry = (carry[0] + long_part, carry[1] + taps_part, carry[2] + skip_part)
        return (carry, (output, gate_grad, signal_grad))
    start = (jnp.zeros((group_count, seq_length), jnp.float32), jnp.zeros((chan_count, tap_count), jnp.float32), jnp.zeros((chan_count,), jnp.float32))
    totals, stacked = lax.scan(one_sequence, start, (signal, gate_input, cotangent))
    factor = 1.0 / math.sqrt(seq_count * seq_length)
    return (stacked[0], stacked[1], stacked[2], totals[0] * factor, (totals[1] * factor).T, totals[2] * factor)
```

```python
import functools
import math

import jax
import jax.numpy as jnp
import ml_dtypes
import numpy as np
from jax import lax
from jax.experimental import pallas as pl
from jax.experimental.pallas import tpu as pltpu
from jax.sharding import PartitionSpec as P

BF16 = jnp.bfloat16
F32 = jnp.float32
VMEM = pl.BlockSpec(memory_space=pltpu.VMEM)
SMEM = pl.BlockSpec(memory_space=pltpu.SMEM)
CHUNK = 32


def split_table(table):
    high = table.astype(ml_dtypes.bfloat16)
    low = (table - high.astype(np.float64)).astype(ml_dtypes.bfloat16)
    return high, low


def dft_tables(block):
    size = 2 * block
    steps = ((2 * np.arange(block)[:, None] + 1) * np.arange(block)[None, :]) % (2 * size)
    angle = steps * (math.pi / size)
    table = np.concatenate([np.cos(angle), -np.sin(angle)], axis=0)
    return split_table(table) + split_table(table.T * (2.0 / size))


def mm(a, b):
    return jnp.dot(a, b, preferred_element_type=F32)


def mm_nt(a, b):
    return lax.dot_general(a, b, (((1,), (1,)), ((), ())), preferred_element_type=F32)


def split(x):
    high = x.astype(BF16)
    return high, (x - high.astype(F32)).astype(BF16)


def inverse(rows_high, rows_low, high, low):
    return mm(rows_high, high) + mm(rows_low, high) + mm(rows_high, low)


def parity(width):
    row = lax.broadcasted_iota(jnp.int32, (CHUNK, width), 0)
    return (1 - 2 * (row % 2)).astype(F32)


def chunks(block, body):
    def step(index, carry):
        body(pl.multiple_of(index * CHUNK, CHUNK))
        return carry

    lax.fori_loop(0, block // CHUNK, step, 0)


def gather_blocks(me_ref, blocks, whole):
    rows = blocks[0].shape[0]
    count = len(blocks)
    for shift, ref in enumerate(blocks):
        source = lax.rem(me_ref[0] + (count - shift), count)
        whole[pl.ds(pl.multiple_of(source * rows, rows), rows), :] = ref[...]


def scatter_blocks(me_ref, whole, blocks):
    rows = blocks[0].shape[0]
    count = len(blocks)
    for shift, ref in enumerate(blocks):
        target = lax.rem(me_ref[0] + shift, count)
        ref[...] = whole[pl.ds(pl.multiple_of(target * rows, rows), rows), :]


def filters_kernel(taps, long_high, long_low, gain, fwd_high, fwd_low, taps_spec, long_spec):
    parts, size, width = long_spec.shape
    block = size // 2
    tap_count = taps.shape[0]
    taps_spec[...] = mm(fwd_high[:, :tap_count], taps[...]) + mm(fwd_low[:, :tap_count], taps[...])
    for d in range(parts):
        rows = pl.ds(d * block, block)
        long_spec[d] = inverse(fwd_high[...], fwd_low[...], long_high[rows, :], long_low[rows, :])
    sign = parity(width)

    def body(at):
        re, im = pl.ds(at, CHUNK), pl.ds(block + at, CHUNK)
        for d in reversed(range(1, parts)):
            long_spec[d, re, :] = long_spec[d, re, :] - sign * long_spec[d - 1, im, :]
            long_spec[d, im, :] = long_spec[d, im, :] + sign * long_spec[d - 1, re, :]
        long_spec[0, re, :] = long_spec[0, re, :] + gain[...]

    chunks(block, body)


def conv_kernel(count, *refs):
    me_ref, blocks, refs = refs[0], refs[1 : 1 + count], refs[1 + count :]
    fwd_high, fwd_low, inv_high, inv_low, taps_spec, long_spec = refs[:6]
    outs, refs = refs[6 : 6 + count], refs[6 + count :]
    near_spec, mixed_spec, whole, series_spec, high, low = refs
    parts, size, width = long_spec.shape
    block = size // 2
    sign = parity(width)
    gather_blocks(me_ref, blocks, whole)
    for i in range(parts):
        x = whole[pl.ds(i * block, block), :]
        series_spec[i] = mm(fwd_high[...], x) + mm(fwd_low[...], x)

    def near(at):
        re, im = pl.ds(at, CHUNK), pl.ds(block + at, CHUNK)
        w_re, w_im = taps_spec[re, :], taps_spec[im, :]
        for i in range(parts):
            s_re, s_im = series_spec[i, re, :], series_spec[i, im, :]
            if i:
                s_re = s_re - sign * series_spec[i - 1, im, :]
                s_im = s_im + sign * series_spec[i - 1, re, :]
            near_spec[i, re, :] = s_re
            near_spec[i, im, :] = s_im
            high[i, re, :], low[i, re, :] = split(w_re * s_re - w_im * s_im)
            high[i, im, :], low[i, im, :] = split(w_re * s_im + w_im * s_re)

    chunks(block, near)
    for i in range(parts):
        x = inverse(inv_high[...], inv_low[...], high[i], low[i]).astype(BF16)
        mixed_spec[i] = mm(fwd_high[...], x) + mm(fwd_low[...], x)

    def far(at):
        re, im = pl.ds(at, CHUNK), pl.ds(block + at, CHUNK)
        for i in range(parts):
            sum_re = sum_im = 0.0
            for d in range(i + 1):
                c_re, c_im = long_spec[d, re, :], long_spec[d, im, :]
                x_re, x_im = mixed_spec[i - d, re, :], mixed_spec[i - d, im, :]
                sum_re = sum_re + (c_re * x_re - c_im * x_im)
                sum_im = sum_im + (c_re * x_im + c_im * x_re)
            high[i, re, :], low[i, re, :] = split(sum_re)
            high[i, im, :], low[i, im, :] = split(sum_im)

    chunks(block, far)
    for i in range(parts):
        whole[pl.ds(i * block, block), :] = inverse(
            inv_high[...], inv_low[...], high[i], low[i]
        ).astype(BF16)
    scatter_blocks(me_ref, whole, outs)


def back_kernel(count, *refs):
    me_ref, blocks, refs = refs[0], refs[1 : 1 + count], refs[1 + count :]
    fwd_high, fwd_low, inv_high, inv_low, taps_spec, long_spec = refs[:6]
    outs, refs = refs[6 : 6 + count], refs[6 + count :]
    grad_spec, back_spec, whole, high, low = refs
    parts, size, width = long_spec.shape
    block = size // 2
    sign = parity(width)
    gather_blocks(me_ref, blocks, whole)
    for i in range(parts):
        x = whole[pl.ds(i * block, block), :]
        grad_spec[i] = mm(fwd_high[...], x) + mm(fwd_low[...], x)

    def far(at):
        re, im = pl.ds(at, CHUNK), pl.ds(block + at, CHUNK)
        for i in range(parts):
            sum_re = sum_im = 0.0
            for d in range(parts - i):
                c_re, c_im = long_spec[d, re, :], long_spec[d, im, :]
                g_re, g_im = grad_spec[i + d, re, :], grad_spec[i + d, im, :]
                sum_re = sum_re + (c_re * g_re + c_im * g_im)
                sum_im = sum_im + (c_re * g_im - c_im * g_re)
            high[i, re, :], low[i, re, :] = split(sum_re)
            high[i, im, :], low[i, im, :] = split(sum_im)

    chunks(block, far)
    for i in range(parts):
        x = inverse(inv_high[...], inv_low[...], high[i], low[i]).astype(BF16)
        back_spec[i] = mm(fwd_high[...], x) + mm(fwd_low[...], x)

    def near(at):
        re, im = pl.ds(at, CHUNK), pl.ds(block + at, CHUNK)
        w_re, w_im = taps_spec[re, :], taps_spec[im, :]
        for i in range(parts):
            b_re, b_im = back_spec[i, re, :], back_spec[i, im, :]
            if i + 1 < parts:
                b_re = b_re + sign * back_spec[i + 1, im, :]
                b_im = b_im - sign * back_spec[i + 1, re, :]
            high[i, re, :], low[i, re, :] = split(w_re * b_re + w_im * b_im)
            high[i, im, :], low[i, im, :] = split(w_re * b_im - w_im * b_re)

    chunks(block, near)
    for i in range(parts):
        whole[pl.ds(i * block, block), :] = inverse(
            inv_high[...], inv_low[...], high[i], low[i]
        ).astype(BF16)
    scatter_blocks(me_ref, whole, outs)


def grads_kernel(
    grad_spec, mixed_spec, back_spec, near_spec, member, fwd_high, fwd_low, inv_high, inv_low,
    long_out, taps_out, skip_out, cross, high, low, total,
):
    parts, size, width = grad_spec.shape
    block = size // 2
    tap_count = taps_out.shape[0]
    sign = parity(width)
    total[...] = jnp.zeros_like(total)

    def products(at):
        re, im = pl.ds(at, CHUNK), pl.ds(block + at, CHUNK)
        p_re, p_im = [], []
        for d in range(parts):
            sum_re = sum_im = 0.0
            for i in range(d, parts):
                g_re, g_im = grad_spec[i, re, :], grad_spec[i, im, :]
                x_re, x_im = mixed_spec[i - d, re, :], mixed_spec[i - d, im, :]
                sum_re = sum_re + (g_re * x_re + g_im * x_im)
                sum_im = sum_im + (g_im * x_re - g_re * x_im)
            p_re.append(sum_re)
            p_im.append(sum_im)
        total[...] += p_re[0]
        for d in range(parts):
            q_re, q_im = p_re[d], p_im[d]
            if d + 1 < parts:
                q_re = q_re + sign * p_im[d + 1]
                q_im = q_im - sign * p_re[d + 1]
            cross[d, re, :], low[d, re, :] = split(q_re)
            cross[d, im, :], low[d, im, :] = split(q_im)
        sum_re = sum_im = 0.0
        for i in range(parts):
            b_re, b_im = back_spec[i, re, :], back_spec[i, im, :]
            s_re, s_im = near_spec[i, re, :], near_spec[i, im, :]
            sum_re = sum_re + (b_re * s_re + b_im * s_im)
            sum_im = sum_im + (b_im * s_re - b_re * s_im)
        high[0, re, :], high[1, re, :] = split(sum_re)
        high[0, im, :], high[1, im, :] = split(sum_im)

    chunks(block, products)
    taps_out[...] = inverse(inv_high[:tap_count, :], inv_low[:tap_count, :], high[0], high[1])
    for d in range(parts):
        summed = mm_nt(member[...], cross[d]) + mm_nt(member[...], low[d])
        s_high, s_low = split(summed * (2.0 / size))
        long_out[:, pl.ds(d * block, block)] = (
            mm(s_high, fwd_high[...]) + mm(s_high, fwd_low[...]) + mm(s_low, fwd_high[...])
        )
    skip_out[...] = jnp.sum(total[...], axis=0, keepdims=True) * (2.0 / size)


def gate_kernel(count, *refs):
    me_ref, blocks, refs = refs[0], refs[1 : 1 + count], refs[1 + count :]
    gating, upstream, output, gate_grad = refs
    width = blocks[0].shape[1]
    for shift, ref in enumerate(blocks):
        source = lax.rem(me_ref[0] + (count - shift), count)
        columns = pl.ds(pl.multiple_of(source * width, width), width)
        conv = ref[...].astype(F32)
        output[:, columns] = (gating[:, columns].astype(F32) * conv).astype(BF16)
        gate_grad[:, columns] = (upstream[:, columns].astype(F32) * conv).astype(BF16)


def place_kernel(count, *refs):
    me_ref, blocks, out = refs[0], refs[1 : 1 + count], refs[-1]
    width = blocks[0].shape[1]
    for shift, ref in enumerate(blocks):
        source = lax.rem(me_ref[0] + (count - shift), count)
        out[:, pl.ds(pl.multiple_of(source * width, width), width)] = ref[...]


def call(kernel, operands, outs, scratch=(), name=None):
    return pl.pallas_call(
        kernel,
        out_shape=outs,
        in_specs=[SMEM if x.dtype == jnp.int32 else VMEM for x in operands],
        out_specs=jax.tree.map(lambda _: VMEM, outs),
        scratch_shapes=[pltpu.VMEM(shape, dtype) for shape, dtype in scratch],
        name=name,
    )(*operands)


def exchange(blocks, axis):
    count = len(blocks)
    return [blocks[0]] + [
        lax.ppermute(blocks[k], axis, [(i, (i + k) % count) for i in range(count)])
        for k in range(1, count)
    ]


def columns_for(rows, me, count):
    width = rows.shape[1] // count
    return [
        lax.dynamic_slice_in_dim(rows, lax.rem(me + k, count) * width, width, 1)
        for k in range(count)
    ]


def in_order(blocks, me):
    count = len(blocks)
    order = lax.rem(me + count - jnp.arange(count), count)
    ordered = jnp.take(jnp.stack(blocks), order, axis=0)
    return jnp.transpose(ordered, (1, 0, 2)).reshape(blocks[0].shape[0], -1)


def sum_over(values, axis):
    if lax.axis_size(axis) != 4:
        return lax.psum(values, axis)

    def other(value, flip):
        return lax.ppermute(value, axis, [(i, i ^ flip) for i in range(4)])

    moved = [[other(v, flip) for v in values] for flip in (1, 2, 3)]
    return tuple((v + a) + (b + c) for v, a, b, c in zip(values, *moved))


def local(signal, gate_input, cotangent, long_filter, short_taps, skip_gain):
    series = signal[0]
    gating = gate_input[0]
    upstream = cotangent[0]
    rows, channels = series.shape
    count = lax.axis_size("ctx")
    me = lax.axis_index("ctx")
    where = me.astype(jnp.int32).reshape(1)
    length = rows * count
    width = channels // count
    groups = long_filter.shape[0]
    tap_count = short_taps.shape[0]
    block = min(length // 4, 512)
    size = 2 * block
    parts = length // block

    grad_gate = (upstream.astype(F32) * gating.astype(F32)).astype(BF16)
    series_in = exchange(columns_for(series, me, count), "ctx")
    grad_in = exchange(columns_for(grad_gate, me, count), "ctx")

    tables = [jnp.asarray(t) for t in dft_tables(block)]
    spread = jnp.repeat(long_filter.T, width // groups, axis=1)
    long_high, long_low = split(spread)
    own_taps = lax.dynamic_slice_in_dim(short_taps, me * width, width, 1)
    spectrum = jax.ShapeDtypeStruct((parts, size, width), F32)
    taps_spec, long_spec = call(
        filters_kernel,
        [own_taps, long_high, long_low, skip_gain[None, :], tables[0], tables[1]],
        [jax.ShapeDtypeStruct((size, width), F32), spectrum],
        name="filters",
    )
    blocks_out = [jax.ShapeDtypeStruct((rows, width), BF16)] * count
    half = ((parts, size, width), BF16)
    *conv, near_spec, mixed_spec = call(
        functools.partial(conv_kernel, count),
        [where, *series_in, *tables, taps_spec, long_spec],
        blocks_out + [spectrum, spectrum],
        [((length, width), BF16), ((parts, size, width), F32), half, half],
        name="conv",
    )
    conv_in = exchange(conv, "ctx")
    *grad, grad_spec, back_spec = call(
        functools.partial(back_kernel, count),
        [where, *grad_in, *tables, taps_spec, long_spec],
        blocks_out + [spectrum, spectrum],
        [((length, width), BF16), half, half],
        name="back",
    )
    signal_in = exchange(grad, "ctx")
    member = jnp.asarray(
        (np.arange(width)[None, :] // (width // groups) == np.arange(groups)[:, None]).astype(
            ml_dtypes.bfloat16
        )
    )
    long_part, taps_part, skip_part = call(
        grads_kernel,
        [grad_spec, mixed_spec, back_spec, near_spec, member, *tables],
        [
            jax.ShapeDtypeStruct((groups, length), F32),
            jax.ShapeDtypeStruct((tap_count, width), F32),
            jax.ShapeDtypeStruct((1, width), F32),
        ],
        [half, ((2, size, width), BF16), half, ((CHUNK, width), F32)],
        name="grads",
    )
    long_sum, taps_sum, skip_sum = sum_over((long_part, taps_part, skip_part), "dp")

    full = jax.ShapeDtypeStruct((rows, channels), BF16)
    if width % 128 == 0:
        output, gate_grad = call(
            functools.partial(gate_kernel, count),
            [where, *conv_in, gating, upstream],
            [full, full],
            name="gate",
        )
        signal_grad = call(
            functools.partial(place_kernel, count), [where, *signal_in], full, name="place"
        )
    else:
        conv_rows = in_order(conv_in, me).astype(F32)
        output = (gating.astype(F32) * conv_rows).astype(BF16)
        gate_grad = (upstream.astype(F32) * conv_rows).astype(BF16)
        signal_grad = in_order(signal_in, me)
    factor = 1.0 / math.sqrt(lax.axis_size("dp") * length)
    return (
        output[None],
        gate_grad[None],
        signal_grad[None],
        long_sum * factor,
        taps_sum * factor,
        skip_sum[0] * factor,
    )


def solution(mesh):
    return jax.shard_map(
        local,
        mesh=mesh,
        in_specs=(
            P("dp", "ctx", None),
            P("dp", "ctx", None),
            P("dp", "ctx", None),
            P("ctx", None),
            P(),
            P("ctx"),
        ),
        out_specs=(
            P("dp", "ctx", None),
            P("dp", "ctx", None),
            P("dp", "ctx", None),
            P("ctx", None),
            P(None, "ctx"),
            P("ctx"),
        ),
        check_vma=False,
    )
```

```python
import functools
import math

import jax
import jax.numpy as jnp
import ml_dtypes
import numpy as np
from jax import lax
from jax.experimental import pallas as pl
from jax.experimental.pallas import tpu as pltpu
from jax.sharding import PartitionSpec as P

BF16 = jnp.bfloat16
F32 = jnp.float32
VMEM = pl.BlockSpec(memory_space=pltpu.VMEM)
SMEM = pl.BlockSpec(memory_space=pltpu.SMEM)
CHUNK = 32


def split_table(table):
    high = table.astype(ml_dtypes.bfloat16)
    low = (table - high.astype(np.float64)).astype(ml_dtypes.bfloat16)
    return high, low


def dft_tables(block):
    size = 2 * block
    steps = ((2 * np.arange(block)[:, None] + 1) * np.arange(block)[None, :]) % (2 * size)
    angle = steps * (math.pi / size)
    table = np.concatenate([np.cos(angle), -np.sin(angle)], axis=0)
    return split_table(table) + split_table(table.T * (2.0 / size))


def mm(a, b):
    return jnp.dot(a, b, preferred_element_type=F32)


def mm_nt(a, b):
    return lax.dot_general(a, b, (((1,), (1,)), ((), ())), preferred_element_type=F32)


def mm_tn(a, b):
    return lax.dot_general(a, b, (((0,), (0,)), ((), ())), preferred_element_type=F32)


def split(x):
    high = x.astype(BF16)
    return high, (x - high.astype(F32)).astype(BF16)


def inverse(rows_high, rows_low, high, low):
    return mm(rows_high, high) + mm(rows_low, high) + mm(rows_high, low)


def parity(width):
    row = lax.broadcasted_iota(jnp.int32, (CHUNK, width), 0)
    return (1 - 2 * (row % 2)).astype(F32)


def chunks(block, body):
    def step(index, carry):
        at = pl.multiple_of(index * CHUNK, CHUNK)
        body(pl.ds(at, CHUNK), pl.ds(block + at, CHUNK))
        return carry

    lax.fori_loop(0, block // CHUNK, step, 0)


def lanes(i, width):
    return slice(i * width, (i + 1) * width)


def place_of(me_ref, step, count, rows, width, block):
    at = lax.rem(me_ref[0] + step + count, count) * rows
    row = pl.multiple_of(lax.rem(at, block), rows)
    column = pl.multiple_of(lax.div(at, block) * width, 128)
    return pl.ds(row, rows), pl.ds(column, width)


def gather_blocks(me_ref, blocks, whole):
    (rows, width), count = blocks[0].shape, len(blocks)
    for shift, ref in enumerate(blocks):
        whole[place_of(me_ref, -shift, count, rows, width, whole.shape[0])] = ref[...]


def scatter_blocks(me_ref, whole, blocks):
    (rows, width), count = blocks[0].shape, len(blocks)
    for shift, ref in enumerate(blocks):
        ref[...] = whole[place_of(me_ref, shift, count, rows, width, whole.shape[0])]


def filters_kernel(
    taps, long_filter, member, gain, fwd_high, fwd_low, inv_high, inv_low,
    taps_spec, long_spec, both_spec, high, low,
):
    size, block = fwd_high.shape
    tap_count, width = taps.shape
    parts = long_spec.shape[1] // width
    sign = parity(width)
    taps_spec[...] = mm(fwd_high[:, :tap_count], taps[...]) + mm(fwd_low[:, :tap_count], taps[...])
    for d in range(parts):
        part_high, part_low = split(long_filter[:, d * block : (d + 1) * block])
        spread_high = mm_tn(part_high, member[...]).astype(BF16)
        spread_low = mm_tn(part_low, member[...]).astype(BF16)
        long_spec[:, lanes(d, width)] = inverse(
            fwd_high[...], fwd_low[...], spread_high, spread_low
        )

    def product(re, im):
        long_spec[re, lanes(0, width)] = long_spec[re, lanes(0, width)] + gain[...]
        w_re, w_im = taps_spec[re, :], taps_spec[im, :]
        for d in range(parts):
            here, last = lanes(d, width), lanes(d - 1, width)
            h_re, h_im = long_spec[re, here], long_spec[im, here]
            if d:
                h_re = h_re - sign * long_spec[im, last]
                h_im = h_im + sign * long_spec[re, last]
            high[re, here], low[re, here] = split(w_re * h_re - w_im * h_im)
            high[im, here], low[im, here] = split(w_re * h_im + w_im * h_re)

    chunks(block, product)
    both = inverse(inv_high[...], inv_low[...], high[...], low[...])
    both_high, both_low = split(both)
    both_spec[...] = inverse(fwd_high[...], fwd_low[...], both_high, both_low)

    def window(re, im):
        for d in reversed(range(1, parts)):
            here, last = lanes(d, width), lanes(d - 1, width)
            both_spec[re, here] = both_spec[re, here] - sign * both_spec[im, last]
            both_spec[im, here] = both_spec[im, here] + sign * both_spec[re, last]

    chunks(block, window)


def conv_kernel(count, backward, *refs):
    me_ref, blocks, refs = refs[0], refs[1 : 1 + count], refs[1 + count :]
    fwd_high, fwd_low, inv_high, inv_low, both_spec = refs[:5]
    outs, (spec, whole, high) = refs[5 : 5 + count], refs[5 + count :]
    size, block = fwd_high.shape
    width = blocks[0].shape[1]
    parts = spec.shape[1] // width
    gather_blocks(me_ref, blocks, whole)
    spec[...] = mm(fwd_high[...], whole[...]) + mm(fwd_low[...], whole[...])

    def product(re, im):
        for i in range(parts):
            sum_re = sum_im = 0.0
            for d in range(parts - i if backward else i + 1):
                there = lanes(i + d if backward else i - d, width)
                c_re, c_im = both_spec[re, lanes(d, width)], both_spec[im, lanes(d, width)]
                x_re, x_im = spec[re, there], spec[im, there]
                if backward:
                    sum_re = sum_re + (c_re * x_re + c_im * x_im)
                    sum_im = sum_im + (c_re * x_im - c_im * x_re)
                else:
                    sum_re = sum_re + (c_re * x_re - c_im * x_im)
                    sum_im = sum_im + (c_re * x_im + c_im * x_re)
            high[re, lanes(i, width)] = sum_re.astype(BF16)
            high[im, lanes(i, width)] = sum_im.astype(BF16)

    chunks(block, product)
    whole[...] = (mm(inv_high[...], high[...]) + mm(inv_low[...], high[...])).astype(BF16)
    scatter_blocks(me_ref, whole, outs)


def grads_kernel(
    grad_spec, series_spec, taps_spec, long_spec, member, fwd_high, fwd_low, inv_high, inv_low,
    out, lag_spec, high, total,
):
    size, block = fwd_high.shape
    groups, width = member.shape
    parts = grad_spec.shape[1] // width
    tap_count = out.shape[0] - 8 - parts * (block // width) * groups
    sign = parity(width)

    def correlate(re, im):
        next_re = next_im = None
        for d in reversed(range(parts)):
            p_re = p_im = 0.0
            for i in range(d, parts):
                here, there = lanes(i, width), lanes(i - d, width)
                g_re, g_im = grad_spec[re, here], grad_spec[im, here]
                x_re, x_im = series_spec[re, there], series_spec[im, there]
                p_re = p_re + (g_re * x_re + g_im * x_im)
                p_im = p_im + (g_im * x_re - g_re * x_im)
            q_re, q_im = p_re, p_im
            if next_re is not None:
                q_re = q_re + sign * next_im
                q_im = q_im - sign * next_re
            high[re, lanes(d, width)] = q_re.astype(BF16)
            high[im, lanes(d, width)] = q_im.astype(BF16)
            next_re, next_im = p_re, p_im

    chunks(block, correlate)
    folded = high[:, : parts * width]
    lags = (mm(inv_high[...], folded) + mm(inv_low[...], folded)).astype(BF16)
    lag_spec[...] = mm(fwd_high[...], lags) + mm(fwd_low[...], lags)
    total[...] = jnp.zeros_like(total)

    def filtered(re, im):
        w_re, w_im = taps_spec[re, :], taps_spec[im, :]
        sum_re = sum_im = 0.0
        for d in range(parts):
            here, after = lanes(d, width), lanes(d + 1, width)
            r_re, r_im = lag_spec[re, here], lag_spec[im, here]
            if d + 1 < parts:
                r_re = r_re + sign * lag_spec[im, after]
                r_im = r_im - sign * lag_spec[re, after]
            h_re, h_im = long_spec[re, here], long_spec[im, here]
            sum_re = sum_re + (h_re * r_re + h_im * r_im)
            sum_im = sum_im + (h_re * r_im - h_im * r_re)
            v_re = w_re * r_re + w_im * r_im
            if d == 0:
                total[...] += v_re
            high[re, here] = v_re.astype(BF16)
            high[im, here] = (w_re * r_im - w_im * r_re).astype(BF16)
        last = lanes(parts, width)
        high[re, last] = sum_re.astype(BF16)
        high[im, last] = sum_im.astype(BF16)

    chunks(block, filtered)
    last = high[:, parts * width :]
    out[:tap_count, :] = mm(inv_high[:tap_count, :], last) + mm(inv_low[:tap_count, :], last)
    skip = jnp.sum(total[...], axis=0, keepdims=True) * (2.0 / size)
    out[pl.ds(tap_count, 8), :] = jnp.broadcast_to(skip, (8, width))
    at = tap_count + 8
    for d in range(parts):
        summed = mm_nt(member[...], high[:, lanes(d, width)]) * (2.0 / size)
        sum_high, sum_low = split(summed)
        part = mm(sum_high, fwd_high[...]) + mm(sum_high, fwd_low[...]) + mm(sum_low, fwd_high[...])
        for piece in range(block // width):
            out[pl.ds(at, groups), :] = part[:, lanes(piece, width)]
            at += groups


def gate_kernel(count, *refs):
    me_ref, blocks, refs = refs[0], refs[1 : 1 + count], refs[1 + count :]
    gating, upstream, output, gate_grad = refs
    width = blocks[0].shape[1]
    for shift, ref in enumerate(blocks):
        source = lax.rem(me_ref[0] + (count - shift), count)
        columns = pl.ds(pl.multiple_of(source * width, width), width)
        conv = ref[...].astype(F32)
        output[:, columns] = (gating[:, columns].astype(F32) * conv).astype(BF16)
        gate_grad[:, columns] = (upstream[:, columns].astype(F32) * conv).astype(BF16)


def place_kernel(count, *refs):
    me_ref, blocks, out = refs[0], refs[1 : 1 + count], refs[-1]
    width = blocks[0].shape[1]
    for shift, ref in enumerate(blocks):
        source = lax.rem(me_ref[0] + (count - shift), count)
        out[:, pl.ds(pl.multiple_of(source * width, width), width)] = ref[...]


def call(kernel, operands, outs, scratch, budget, micros, name):
    moved = sum(math.prod(x.shape) * x.dtype.itemsize for x in [*operands, *outs])
    return pl.pallas_call(
        kernel,
        out_shape=outs,
        in_specs=[SMEM if x.dtype == jnp.int32 else VMEM for x in operands],
        out_specs=[VMEM for _ in outs],
        scratch_shapes=[pltpu.VMEM(shape, dtype) for shape, dtype in scratch],
        compiler_params=pltpu.CompilerParams(vmem_limit_bytes=budget),
        cost_estimate=pl.CostEstimate(
            flops=int(micros * 1e9), transcendentals=0, bytes_accessed=moved
        ),
        name=name,
    )(*operands)


def exchange(blocks, axis):
    count = len(blocks)
    return [blocks[0]] + [
        lax.ppermute(blocks[k], axis, [(i, (i + k) % count) for i in range(count)])
        for k in range(1, count)
    ]


def columns_for(rows, me, count):
    width = rows.shape[1] // count
    return [
        lax.dynamic_slice_in_dim(rows, lax.rem(me + k, count) * width, width, 1)
        for k in range(count)
    ]


def in_order(blocks, me):
    count = len(blocks)
    order = lax.rem(me + count - jnp.arange(count), count)
    ordered = jnp.take(jnp.stack(blocks), order, axis=0)
    return jnp.transpose(ordered, (1, 0, 2)).reshape(blocks[0].shape[0], -1)


def sum_over(value, axis):
    if lax.axis_size(axis) != 4:
        return lax.psum(value, axis)
    a, b, c = (lax.ppermute(value, axis, [(i, i ^ flip) for i in range(4)]) for flip in (1, 2, 3))
    return (value + a) + (b + c)


def local(signal, gate_input, cotangent, long_filter, short_taps, skip_gain):
    series = signal[0]
    gating = gate_input[0]
    upstream = cotangent[0]
    rows, channels = series.shape
    count = lax.axis_size("ctx")
    me = lax.axis_index("ctx")
    where = me.astype(jnp.int32).reshape(1)
    length = rows * count
    width = channels // count
    padded = -(-width // 128) * 128
    groups = long_filter.shape[0]
    tap_count = short_taps.shape[0]
    block = min(length // 4, 512)
    size = 2 * block
    parts = length // block

    def pad(x):
        return jnp.pad(x, ((0, 0), (0, padded - width))) if padded > width else x

    def trim(blocks):
        return [x[:, :width] if padded > width else x for x in blocks]

    grad_gate = (upstream.astype(F32) * gating.astype(F32)).astype(BF16)
    series_in = exchange(columns_for(series, me, count), "ctx")
    grad_in = exchange(columns_for(grad_gate, me, count), "ctx")

    tables = [jnp.asarray(t) for t in dft_tables(block)]
    channel = np.arange(padded)[None, :]
    of_group = (channel // (width // groups) == np.arange(groups)[:, None]) & (channel < width)
    member = jnp.asarray(of_group.astype(ml_dtypes.bfloat16))
    own_taps = pad(lax.dynamic_slice_in_dim(short_taps, me * width, width, 1))
    spectrum = (size, parts * padded)
    spectrum_out = jax.ShapeDtypeStruct(spectrum, F32)
    budget = 10 * 4 * math.prod(spectrum)
    taps_spec, long_spec, both_spec = call(
        filters_kernel,
        [own_taps, long_filter, member, pad(skip_gain[None, :]), *tables],
        [jax.ShapeDtypeStruct((size, padded), F32), spectrum_out, spectrum_out],
        [(spectrum, BF16), (spectrum, BF16)],
        budget,
        5,
        "filters",
    )

    def convolve(blocks, backward, name):
        *outs, spec = call(
            functools.partial(conv_kernel, count, backward),
            [where, *[pad(x) for x in blocks], *tables, both_spec],
            [jax.ShapeDtypeStruct((rows, padded), BF16)] * count + [spectrum_out],
            [((block, parts * padded), BF16), (spectrum, BF16)],
            budget,
            4,
            name,
        )
        return trim(outs), spec

    conv, series_spec = convolve(series_in, False, "conv")
    conv_in = exchange(conv, "ctx")
    grad_in, conv = lax.optimization_barrier((grad_in, conv))
    grad, grad_spec = convolve(grad_in, True, "back")
    signal_in = exchange(grad, "ctx")
    pieces = parts * (block // padded)
    (partial,) = call(
        grads_kernel,
        [grad_spec, series_spec, taps_spec, long_spec, member, *tables],
        [jax.ShapeDtypeStruct((tap_count + 8 + pieces * groups, padded), F32)],
        [(spectrum, F32), ((size, (parts + 1) * padded), BF16), ((CHUNK, padded), F32)],
        budget,
        5,
        "grads",
    )
    total = sum_over(partial, "dp") * (1.0 / math.sqrt(lax.axis_size("dp") * length))
    taps_grad = total[:tap_count, :width]
    skip_grad = total[tap_count, :width]
    long_grad = total[tap_count + 8 :].reshape(pieces, groups, padded)
    long_grad = jnp.transpose(long_grad, (1, 0, 2)).reshape(groups, length)

    full = jax.ShapeDtypeStruct((rows, channels), BF16)
    if width % 128 == 0:
        output, gate_grad = call(
            functools.partial(gate_kernel, count),
            [where, *conv_in, gating, upstream],
            [full, full],
            [],
            budget,
            1,
            "gate",
        )
        (signal_grad,) = call(
            functools.partial(place_kernel, count),
            [where, *signal_in],
            [full],
            [],
            budget,
            1,
            "place",
        )
    else:
        conv_rows = in_order(conv_in, me).astype(F32)
        output = (gating.astype(F32) * conv_rows).astype(BF16)
        gate_grad = (upstream.astype(F32) * conv_rows).astype(BF16)
        signal_grad = in_order(signal_in, me)
    return (output[None], gate_grad[None], signal_grad[None], long_grad, taps_grad, skip_grad)


def solution(mesh):
    return jax.shard_map(
        local,
        mesh=mesh,
        in_specs=(
            P("dp", "ctx", None),
            P("dp", "ctx", None),
            P("dp", "ctx", None),
            P("ctx", None),
            P(),
            P("ctx"),
        ),
        out_specs=(
            P("dp", "ctx", None),
            P("dp", "ctx", None),
            P("dp", "ctx", None),
            P("ctx", None),
            P(None, "ctx"),
            P("ctx"),
        ),
        check_vma=False,
    )
```

```python
import functools
import math

import jax
import jax.numpy as jnp
import ml_dtypes
import numpy as np
from jax import lax
from jax.experimental import pallas as pl
from jax.experimental.pallas import tpu as pltpu
from jax.sharding import PartitionSpec as P

BF16 = jnp.bfloat16
F32 = jnp.float32
VMEM = pl.BlockSpec(memory_space=pltpu.VMEM)
SMEM = pl.BlockSpec(memory_space=pltpu.SMEM)
CHUNK = 32


def split_table(table):
    high = table.astype(ml_dtypes.bfloat16)
    low = (table - high.astype(np.float64)).astype(ml_dtypes.bfloat16)
    return high, low


def dft_tables(block):
    size = 2 * block
    steps = ((2 * np.arange(block)[:, None] + 1) * np.arange(block)[None, :]) % (2 * size)
    angle = steps * (math.pi / size)
    table = np.concatenate([np.cos(angle), -np.sin(angle)], axis=0)
    return split_table(table) + split_table(table.T * (2.0 / size))


def mm(a, b):
    return jnp.dot(a, b, preferred_element_type=F32)


def mm_nt(a, b):
    return lax.dot_general(a, b, (((1,), (1,)), ((), ())), preferred_element_type=F32)


def mm_tn(a, b):
    return lax.dot_general(a, b, (((0,), (0,)), ((), ())), preferred_element_type=F32)


def split(x):
    high = x.astype(BF16)
    return high, (x - high.astype(F32)).astype(BF16)


def inverse(rows_high, rows_low, high, low):
    return mm(rows_high, high) + mm(rows_low, high) + mm(rows_high, low)


def parity(width):
    row = lax.broadcasted_iota(jnp.int32, (CHUNK, width), 0)
    return (1 - 2 * (row % 2)).astype(F32)


def chunks(block, body):
    def step(index, carry):
        at = pl.multiple_of(index * CHUNK, CHUNK)
        body(pl.ds(at, CHUNK), pl.ds(block + at, CHUNK))
        return carry

    lax.fori_loop(0, block // CHUNK, step, 0)


def lanes(i, width):
    return slice(i * width, (i + 1) * width)


def place_of(me_ref, step, count, rows, width, block):
    at = lax.rem(me_ref[0] + step + count, count) * rows
    row = pl.multiple_of(lax.rem(at, block), rows)
    column = pl.multiple_of(lax.div(at, block) * width, 128)
    return pl.ds(row, rows), pl.ds(column, width)


def gather_blocks(me_ref, blocks, which, whole):
    (rows, width), count = blocks[0].shape, len(blocks)
    rows //= 2
    for shift, ref in enumerate(blocks):
        at = place_of(me_ref, -shift, count, rows, width, whole.shape[0])
        whole[at] = ref[which * rows : (which + 1) * rows, :]


def scatter_blocks(me_ref, whole, which, blocks):
    (rows, width), count = blocks[0].shape, len(blocks)
    rows //= 2
    for shift, ref in enumerate(blocks):
        ref[which * rows : (which + 1) * rows, :] = whole[place_of(me_ref, shift, count, rows, width, whole.shape[0])]


def filters_kernel(
    taps, long_filter, member, gain, fwd_high, fwd_low, inv_high, inv_low,
    taps_spec, long_spec, both_spec, high, low,
):
    size, block = fwd_high.shape
    tap_count, width = taps.shape
    parts = long_spec.shape[1] // width
    sign = parity(width)
    taps_spec[...] = mm(fwd_high[:, :tap_count], taps[...]) + mm(fwd_low[:, :tap_count], taps[...])
    for d in range(parts):
        part_high, part_low = split(long_filter[:, d * block : (d + 1) * block])
        spread_high = mm_tn(part_high, member[...]).astype(BF16)
        spread_low = mm_tn(part_low, member[...]).astype(BF16)
        long_spec[:, lanes(d, width)] = inverse(
            fwd_high[...], fwd_low[...], spread_high, spread_low
        )

    def product(re, im):
        long_spec[re, lanes(0, width)] = long_spec[re, lanes(0, width)] + gain[...]
        w_re, w_im = taps_spec[re, :], taps_spec[im, :]
        for d in range(parts):
            here, last = lanes(d, width), lanes(d - 1, width)
            h_re, h_im = long_spec[re, here], long_spec[im, here]
            if d:
                h_re = h_re - sign * long_spec[im, last]
                h_im = h_im + sign * long_spec[re, last]
            high[re, here], low[re, here] = split(w_re * h_re - w_im * h_im)
            high[im, here], low[im, here] = split(w_re * h_im + w_im * h_re)

    chunks(block, product)
    both = inverse(inv_high[...], inv_low[...], high[...], low[...])
    both_high, both_low = split(both)
    both_spec[...] = inverse(fwd_high[...], fwd_low[...], both_high, both_low)

    def window(re, im):
        for d in reversed(range(1, parts)):
            here, last = lanes(d, width), lanes(d - 1, width)
            both_spec[re, here] = both_spec[re, here] - sign * both_spec[im, last]
            both_spec[im, here] = both_spec[im, here] + sign * both_spec[re, last]

    chunks(block, window)


def conv_kernel(count, *refs):
    me_ref, blocks, refs = refs[0], refs[1 : 1 + count], refs[1 + count :]
    fwd_high, fwd_low, inv_high, inv_low, both_spec = refs[:5]
    outs, (series_spec, grad_spec, whole, high) = refs[5 : 5 + count], refs[5 + count :]
    size, block = fwd_high.shape
    width = blocks[0].shape[1]
    parts = series_spec.shape[1] // width

    for which, spec in enumerate((series_spec, grad_spec)):
        backward = which == 1
        gather_blocks(me_ref, blocks, which, whole)
        spec[...] = mm(fwd_high[...], whole[...]) + mm(fwd_low[...], whole[...])

        def product(re, im):
            for i in range(parts):
                sum_re = sum_im = 0.0
                for d in range(parts - i if backward else i + 1):
                    there = lanes(i + d if backward else i - d, width)
                    c_re, c_im = both_spec[re, lanes(d, width)], both_spec[im, lanes(d, width)]
                    x_re, x_im = spec[re, there], spec[im, there]
                    if backward:
                        sum_re = sum_re + (c_re * x_re + c_im * x_im)
                        sum_im = sum_im + (c_re * x_im - c_im * x_re)
                    else:
                        sum_re = sum_re + (c_re * x_re - c_im * x_im)
                        sum_im = sum_im + (c_re * x_im + c_im * x_re)
                high[re, lanes(i, width)] = sum_re.astype(BF16)
                high[im, lanes(i, width)] = sum_im.astype(BF16)

        chunks(block, product)
        whole[...] = (mm(inv_high[...], high[...]) + mm(inv_low[...], high[...])).astype(BF16)
        scatter_blocks(me_ref, whole, which, outs)


def grads_kernel(
    grad_spec, series_spec, taps_spec, long_spec, member, fwd_high, fwd_low, inv_high, inv_low,
    out, lag_spec, high, total,
):
    size, block = fwd_high.shape
    groups, width = member.shape
    parts = grad_spec.shape[1] // width
    tap_count = out.shape[0] - 8 - parts * (block // width) * groups
    sign = parity(width)

    def correlate(re, im):
        next_re = next_im = None
        for d in reversed(range(parts)):
            p_re = p_im = 0.0
            for i in range(d, parts):
                here, there = lanes(i, width), lanes(i - d, width)
                g_re, g_im = grad_spec[re, here], grad_spec[im, here]
                x_re, x_im = series_spec[re, there], series_spec[im, there]
                p_re = p_re + (g_re * x_re + g_im * x_im)
                p_im = p_im + (g_im * x_re - g_re * x_im)
            q_re, q_im = p_re, p_im
            if next_re is not None:
                q_re = q_re + sign * next_im
                q_im = q_im - sign * next_re
            high[re, lanes(d, width)] = q_re.astype(BF16)
            high[im, lanes(d, width)] = q_im.astype(BF16)
            next_re, next_im = p_re, p_im

    chunks(block, correlate)
    folded = high[:, : parts * width]
    lags = (mm(inv_high[...], folded) + mm(inv_low[...], folded)).astype(BF16)
    lag_spec[...] = mm(fwd_high[...], lags) + mm(fwd_low[...], lags)
    total[...] = jnp.zeros_like(total)

    def filtered(re, im):
        w_re, w_im = taps_spec[re, :], taps_spec[im, :]
        sum_re = sum_im = 0.0
        for d in range(parts):
            here, after = lanes(d, width), lanes(d + 1, width)
            r_re, r_im = lag_spec[re, here], lag_spec[im, here]
            if d + 1 < parts:
                r_re = r_re + sign * lag_spec[im, after]
                r_im = r_im - sign * lag_spec[re, after]
            h_re, h_im = long_spec[re, here], long_spec[im, here]
            sum_re = sum_re + (h_re * r_re + h_im * r_im)
            sum_im = sum_im + (h_re * r_im - h_im * r_re)
            v_re = w_re * r_re + w_im * r_im
            if d == 0:
                total[...] += v_re
            high[re, here] = v_re.astype(BF16)
            high[im, here] = (w_re * r_im - w_im * r_re).astype(BF16)
        last = lanes(parts, width)
        high[re, last] = sum_re.astype(BF16)
        high[im, last] = sum_im.astype(BF16)

    chunks(block, filtered)
    last = high[:, parts * width :]
    out[:tap_count, :] = mm(inv_high[:tap_count, :], last) + mm(inv_low[:tap_count, :], last)
    skip = jnp.sum(total[...], axis=0, keepdims=True) * (2.0 / size)
    out[pl.ds(tap_count, 8), :] = jnp.broadcast_to(skip, (8, width))
    at = tap_count + 8
    for d in range(parts):
        summed = mm_nt(member[...], high[:, lanes(d, width)]) * (2.0 / size)
        sum_high, sum_low = split(summed)
        part = mm(sum_high, fwd_high[...]) + mm(sum_high, fwd_low[...]) + mm(sum_low, fwd_high[...])
        for piece in range(block // width):
            out[pl.ds(at, groups), :] = part[:, lanes(piece, width)]
            at += groups


def prepare_kernel(count, me_ref, series, gating, upstream, *refs):
    outs, (gate_held, up_held, series_sem, gate_sem, up_sem) = refs[:count], refs[count:]
    rows, channels = series.shape
    width = channels // count

    def columns(shift):
        target = lax.rem(me_ref[0] + shift, count)
        return pl.ds(pl.multiple_of(target * width, width), width)

    copies = []
    for shift, ref in enumerate(outs):
        here = columns(shift)
        copies.append(
            (
                pltpu.make_async_copy(gating.at[:, here], gate_held.at[shift], gate_sem.at[shift]),
                pltpu.make_async_copy(upstream.at[:, here], up_held.at[shift], up_sem.at[shift]),
                pltpu.make_async_copy(series.at[:, here], ref.at[:rows, :], series_sem.at[shift]),
            )
        )
    for group in copies:
        for copy in group:
            copy.start()
    for shift, ref in enumerate(outs):
        for copy in copies[shift]:
            copy.wait()
        product = up_held[shift].astype(F32) * gate_held[shift].astype(F32)
        ref[rows:, :] = product.astype(BF16)


def finish_kernel(scale, first, second, third, fourth, long_grad, taps_grad, skip_grad):
    groups, length = long_grad.shape
    tap_count, width = taps_grad.shape
    padded = first.shape[1]

    def total(at, rows):
        here = pl.ds(at, rows)
        return ((first[here, :] + second[here, :]) + (third[here, :] + fourth[here, :])) * scale

    taps_grad[...] = total(0, tap_count)[:, :width]
    skip_grad[...] = total(tap_count, 8)[:1, :width]
    for piece in range(length // padded):
        long_grad[:, lanes(piece, padded)] = total(tap_count + 8 + piece * groups, groups)


def gate_kernel(count, *refs):
    me_ref, blocks, refs = refs[0], refs[1 : 1 + count], refs[1 + count :]
    gating, upstream, output, gate_grad, signal_grad = refs
    rows = gating.shape[0]
    width = blocks[0].shape[1]
    for shift, ref in enumerate(blocks):
        source = lax.rem(me_ref[0] + (count - shift), count)
        columns = pl.ds(pl.multiple_of(source * width, width), width)
        conv = ref[:rows, :].astype(F32)
        output[:, columns] = (gating[:, columns].astype(F32) * conv).astype(BF16)
        gate_grad[:, columns] = (upstream[:, columns].astype(F32) * conv).astype(BF16)
        signal_grad[:, columns] = ref[rows:, :]


def call(kernel, operands, outs, scratch, budget, micros, name, space=pltpu.VMEM):
    moved = sum(math.prod(x.shape) * x.dtype.itemsize for x in [*operands, *outs])
    return pl.pallas_call(
        kernel,
        out_shape=outs,
        in_specs=[
            SMEM if x.dtype == jnp.int32 else pl.BlockSpec(memory_space=space) for x in operands
        ],
        out_specs=[VMEM for _ in outs],
        scratch_shapes=[pltpu.VMEM(*x) if isinstance(x, tuple) else x for x in scratch],
        compiler_params=pltpu.CompilerParams(vmem_limit_bytes=budget),
        cost_estimate=pl.CostEstimate(
            flops=int(micros * 1e9), transcendentals=0, bytes_accessed=moved
        ),
        name=name,
    )(*operands)


def exchange(blocks, axis, shifts):
    count = len(blocks)
    moved = list(blocks)
    for k in shifts:
        moved[k] = lax.ppermute(blocks[k], axis, [(i, (i + k) % count) for i in range(count)])
    return moved


def columns_for(rows, me, count):
    width = rows.shape[1] // count
    return [
        lax.dynamic_slice_in_dim(rows, lax.rem(me + k, count) * width, width, 1)
        for k in range(count)
    ]


def in_order(blocks, me):
    count = len(blocks)
    order = lax.rem(me + count - jnp.arange(count), count)
    ordered = jnp.take(jnp.stack(blocks), order, axis=0)
    return jnp.transpose(ordered, (1, 0, 2)).reshape(blocks[0].shape[0], -1)


def shares(value, axis):
    return [value] + [lax.ppermute(value, axis, [(i, i ^ flip) for i in range(4)]) for flip in (1, 2, 3)]


def local(signal, gate_input, cotangent, long_filter, short_taps, skip_gain):
    series = signal[0]
    gating = gate_input[0]
    upstream = cotangent[0]
    rows, channels = series.shape
    count = lax.axis_size("ctx")
    me = lax.axis_index("ctx")
    where = me.astype(jnp.int32).reshape(1)
    length = rows * count
    width = channels // count
    padded = -(-width // 128) * 128
    groups = long_filter.shape[0]
    tap_count = short_taps.shape[0]
    block = min(length // 4, 512)
    size = 2 * block
    parts = length // block

    def pad(x):
        return jnp.pad(x, ((0, 0), (0, padded - width))) if padded > width else x

    def trim(blocks):
        return [x[:, :width] if padded > width else x for x in blocks]

    spectrum = (size, parts * padded)
    spectrum_out = jax.ShapeDtypeStruct(spectrum, F32)
    budget = 10 * 4 * math.prod(spectrum)
    tables = [jnp.asarray(t) for t in dft_tables(block)]
    channel = np.arange(padded)[None, :]
    of_group = (channel // (width // groups) == np.arange(groups)[:, None]) & (channel < width)
    member = jnp.asarray(of_group.astype(ml_dtypes.bfloat16))
    if width % 128 == 0:
        sent = call(
            functools.partial(prepare_kernel, count),
            [where, series, gating, upstream],
            [jax.ShapeDtypeStruct((2 * rows, width), BF16)] * count,
            [((count, rows, width), BF16)] * 2 + [pltpu.SemaphoreType.DMA((count,))] * 3,
            None,
            1,
            "prepare",
            pltpu.HBM,
        )
    else:
        grad_gate = (upstream.astype(F32) * gating.astype(F32)).astype(BF16)
        sent = columns_for(jnp.concatenate([series, grad_gate]), me, count)
    received = [pad(x) for x in exchange(sent, "ctx", range(1, count))]
    own_taps = pad(lax.dynamic_slice_in_dim(short_taps, me * width, width, 1))
    taps_spec, long_spec, both_spec = call(
        filters_kernel,
        [own_taps, long_filter, member, pad(skip_gain[None, :]), *tables],
        [jax.ShapeDtypeStruct((size, padded), F32), spectrum_out, spectrum_out],
        [(spectrum, BF16), (spectrum, BF16)],
        budget,
        5,
        "filters",
    )

    *outs, series_spec, grad_spec = call(
        functools.partial(conv_kernel, count),
        [where, *received, *tables, both_spec],
        [jax.ShapeDtypeStruct((2 * rows, padded), BF16)] * count + [spectrum_out] * 2,
        [((block, parts * padded), BF16), (spectrum, BF16)],
        budget,
        8,
        "conv",
    )
    outs = trim(outs)
    early, late = [1, 7], []
    returned = exchange(outs, "ctx", [1, 7, 4, 3, 5, 2, 6] if count == 8 else range(1, count))
    *waited, grad_spec = lax.optimization_barrier([returned[k] for k in early] + [grad_spec])
    for k, value in zip(early, waited):
        returned[k] = value
    pieces = parts * (block // padded)
    (partial,) = call(
        grads_kernel,
        [grad_spec, series_spec, taps_spec, long_spec, member, *tables],
        [jax.ShapeDtypeStruct((tap_count + 8 + pieces * groups, padded), F32)],
        [(spectrum, F32), ((size, (parts + 1) * padded), BF16), ((CHUNK, padded), F32)],
        budget,
        5,
        "grads",
    )
    scale = 1.0 / math.sqrt(lax.axis_size("dp") * length)
    if lax.axis_size("dp") == 4:
        partials = shares(partial, "dp")
    else:
        partials = [lax.psum(partial, "dp")] + [jnp.zeros_like(partial)] * 3
    long_grad, taps_grad, skip_grad = call(
        functools.partial(finish_kernel, scale),
        partials,
        [
            jax.ShapeDtypeStruct((groups, length), F32),
            jax.ShapeDtypeStruct((tap_count, width), F32),
            jax.ShapeDtypeStruct((1, width), F32),
        ],
        [],
        budget,
        1,
        "finish",
    )

    full = jax.ShapeDtypeStruct((rows, channels), BF16)
    if width % 128 == 0:
        output, gate_grad, signal_grad = call(
            functools.partial(gate_kernel, count),
            [where, *returned, gating, upstream],
            [full, full, full],
            [],
            budget,
            1,
            "gate",
        )
    else:
        conv_rows, signal_grad = jnp.split(in_order(returned, me), 2)
        conv_rows = conv_rows.astype(F32)
        output = (gating.astype(F32) * conv_rows).astype(BF16)
        gate_grad = (upstream.astype(F32) * conv_rows).astype(BF16)
    return (output[None], gate_grad[None], signal_grad[None], long_grad, taps_grad, skip_grad[0])


def solution(mesh):
    return jax.shard_map(
        local,
        mesh=mesh,
        in_specs=(
            P("dp", "ctx", None),
            P("dp", "ctx", None),
            P("dp", "ctx", None),
            P("ctx", None),
            P(),
            P("ctx"),
        ),
        out_specs=(
            P("dp", "ctx", None),
            P("dp", "ctx", None),
            P("dp", "ctx", None),
            P("ctx", None),
            P(None, "ctx"),
            P("ctx"),
        ),
        check_vma=False,
    )
```

```python
import functools
import math

import jax
import jax.numpy as jnp
import ml_dtypes
import numpy as np
from jax import lax
from jax.experimental import pallas as pl
from jax.experimental.pallas import tpu as pltpu
from jax.sharding import PartitionSpec as P

BF16 = jnp.bfloat16
F32 = jnp.float32
VMEM = pl.BlockSpec(memory_space=pltpu.VMEM)
SMEM = pl.BlockSpec(memory_space=pltpu.SMEM)
CHUNK = 32


def split_table(table):
    high = table.astype(ml_dtypes.bfloat16)
    low = (table - high.astype(np.float64)).astype(ml_dtypes.bfloat16)
    return high, low


def dft_tables(block):
    size = 2 * block
    steps = ((2 * np.arange(block)[:, None] + 1) * np.arange(block)[None, :]) % (2 * size)
    angle = steps * (math.pi / size)
    table = np.concatenate([np.cos(angle), -np.sin(angle)], axis=0)
    return split_table(table) + split_table(table.T * (2.0 / size))


def mm(a, b):
    return jnp.dot(a, b, preferred_element_type=F32)


def mm_nt(a, b):
    return lax.dot_general(a, b, (((1,), (1,)), ((), ())), preferred_element_type=F32)


def mm_tn(a, b):
    return lax.dot_general(a, b, (((0,), (0,)), ((), ())), preferred_element_type=F32)


def split(x):
    high = x.astype(BF16)
    return high, (x - high.astype(F32)).astype(BF16)


def inverse(rows_high, rows_low, high, low):
    return mm(rows_high, high) + mm(rows_low, high) + mm(rows_high, low)


def parity(width):
    row = lax.broadcasted_iota(jnp.int32, (CHUNK, width), 0)
    return (1 - 2 * (row % 2)).astype(F32)


def chunks(block, body):
    def step(index, carry):
        at = pl.multiple_of(index * CHUNK, CHUNK)
        body(pl.ds(at, CHUNK), pl.ds(block + at, CHUNK))
        return carry

    lax.fori_loop(0, block // CHUNK, step, 0)


def lanes(i, width):
    return slice(i * width, (i + 1) * width)


def place_of(me_ref, step, count, rows, width, block):
    at = lax.rem(me_ref[0] + step + count, count) * rows
    row = pl.multiple_of(lax.rem(at, block), rows)
    column = pl.multiple_of(lax.div(at, block) * width, 128)
    return pl.ds(row, rows), pl.ds(column, width)


def gather_blocks(me_ref, order, blocks, which, whole):
    (rows, width), count = blocks[0].shape, len(blocks)
    rows //= 2
    for shift, ref in zip(order, blocks):
        at = place_of(me_ref, -shift, count, rows, width, whole.shape[0])
        whole[at] = ref[which * rows : (which + 1) * rows, :]


def scatter_blocks(me_ref, whole, which, blocks):
    (rows, width), count = blocks[0].shape, len(blocks)
    rows //= 2
    for shift, ref in enumerate(blocks):
        ref[which * rows : (which + 1) * rows, :] = whole[place_of(me_ref, shift, count, rows, width, whole.shape[0])]


def filters_kernel(
    taps, long_filter, member, gain, fwd_high, fwd_low, inv_high, inv_low,
    taps_spec, long_spec, both_spec, high, low,
):
    size, block = fwd_high.shape
    tap_count, width = taps.shape
    parts = long_spec.shape[1] // width
    sign = parity(width)
    taps_spec[...] = mm(fwd_high[:, :tap_count], taps[...]) + mm(fwd_low[:, :tap_count], taps[...])
    for d in range(parts):
        part_high, part_low = split(long_filter[:, d * block : (d + 1) * block])
        spread_high = mm_tn(part_high, member[...]).astype(BF16)
        spread_low = mm_tn(part_low, member[...]).astype(BF16)
        long_spec[:, lanes(d, width)] = inverse(
            fwd_high[...], fwd_low[...], spread_high, spread_low
        )

    def product(re, im):
        long_spec[re, lanes(0, width)] = long_spec[re, lanes(0, width)] + gain[...]
        w_re, w_im = taps_spec[re, :], taps_spec[im, :]
        for d in range(parts):
            here, last = lanes(d, width), lanes(d - 1, width)
            h_re, h_im = long_spec[re, here], long_spec[im, here]
            if d:
                h_re = h_re - sign * long_spec[im, last]
                h_im = h_im + sign * long_spec[re, last]
            high[re, here], low[re, here] = split(w_re * h_re - w_im * h_im)
            high[im, here], low[im, here] = split(w_re * h_im + w_im * h_re)

    chunks(block, product)
    both = inverse(inv_high[...], inv_low[...], high[...], low[...])
    both_high, both_low = split(both)
    both_spec[...] = inverse(fwd_high[...], fwd_low[...], both_high, both_low)

    def window(re, im):
        for d in reversed(range(1, parts)):
            here, last = lanes(d, width), lanes(d - 1, width)
            both_spec[re, here] = both_spec[re, here] - sign * both_spec[im, last]
            both_spec[im, here] = both_spec[im, here] + sign * both_spec[re, last]

    chunks(block, window)


def conv_kernel(order, *refs):
    count = len(order)
    me_ref, blocks, refs = refs[0], refs[1 : 1 + count], refs[1 + count :]
    fwd_high, fwd_low, inv_high, inv_low, both_spec = refs[:5]
    outs, (series_spec, grad_spec, whole, high) = refs[5 : 5 + count], refs[5 + count :]
    size, block = fwd_high.shape
    width = blocks[0].shape[1]
    parts = series_spec.shape[1] // width

    for which, spec in enumerate((series_spec, grad_spec)):
        backward = which == 1
        gather_blocks(me_ref, order, blocks, which, whole)
        spec[...] = mm(fwd_high[...], whole[...]) + mm(fwd_low[...], whole[...])

        def product(re, im):
            for i in range(parts):
                sum_re = sum_im = 0.0
                for d in range(parts - i if backward else i + 1):
                    there = lanes(i + d if backward else i - d, width)
                    c_re, c_im = both_spec[re, lanes(d, width)], both_spec[im, lanes(d, width)]
                    x_re, x_im = spec[re, there], spec[im, there]
                    if backward:
                        sum_re = sum_re + (c_re * x_re + c_im * x_im)
                        sum_im = sum_im + (c_re * x_im - c_im * x_re)
                    else:
                        sum_re = sum_re + (c_re * x_re - c_im * x_im)
                        sum_im = sum_im + (c_re * x_im + c_im * x_re)
                high[re, lanes(i, width)] = sum_re.astype(BF16)
                high[im, lanes(i, width)] = sum_im.astype(BF16)

        chunks(block, product)
        whole[...] = (mm(inv_high[...], high[...]) + mm(inv_low[...], high[...])).astype(BF16)
        scatter_blocks(me_ref, whole, which, outs)


def grads_kernel(
    grad_spec, series_spec, taps_spec, long_spec, member, fwd_high, fwd_low, inv_high, inv_low,
    out, lag_spec, high, total,
):
    size, block = fwd_high.shape
    groups, width = member.shape
    parts = grad_spec.shape[1] // width
    tap_count = out.shape[0] - 8 - parts * (block // width) * groups
    sign = parity(width)

    def correlate(re, im):
        next_re = next_im = None
        for d in reversed(range(parts)):
            p_re = p_im = 0.0
            for i in range(d, parts):
                here, there = lanes(i, width), lanes(i - d, width)
                g_re, g_im = grad_spec[re, here], grad_spec[im, here]
                x_re, x_im = series_spec[re, there], series_spec[im, there]
                p_re = p_re + (g_re * x_re + g_im * x_im)
                p_im = p_im + (g_im * x_re - g_re * x_im)
            q_re, q_im = p_re, p_im
            if next_re is not None:
                q_re = q_re + sign * next_im
                q_im = q_im - sign * next_re
            high[re, lanes(d, width)] = q_re.astype(BF16)
            high[im, lanes(d, width)] = q_im.astype(BF16)
            next_re, next_im = p_re, p_im

    chunks(block, correlate)
    folded = high[:, : parts * width]
    lags = (mm(inv_high[...], folded) + mm(inv_low[...], folded)).astype(BF16)
    lag_spec[...] = mm(fwd_high[...], lags) + mm(fwd_low[...], lags)
    total[...] = jnp.zeros_like(total)

    def filtered(re, im):
        w_re, w_im = taps_spec[re, :], taps_spec[im, :]
        sum_re = sum_im = 0.0
        for d in range(parts):
            here, after = lanes(d, width), lanes(d + 1, width)
            r_re, r_im = lag_spec[re, here], lag_spec[im, here]
            if d + 1 < parts:
                r_re = r_re + sign * lag_spec[im, after]
                r_im = r_im - sign * lag_spec[re, after]
            h_re, h_im = long_spec[re, here], long_spec[im, here]
            sum_re = sum_re + (h_re * r_re + h_im * r_im)
            sum_im = sum_im + (h_re * r_im - h_im * r_re)
            v_re = w_re * r_re + w_im * r_im
            if d == 0:
                total[...] += v_re
            high[re, here] = v_re.astype(BF16)
            high[im, here] = (w_re * r_im - w_im * r_re).astype(BF16)
        last = lanes(parts, width)
        high[re, last] = sum_re.astype(BF16)
        high[im, last] = sum_im.astype(BF16)

    chunks(block, filtered)
    last = high[:, parts * width :]
    out[:tap_count, :] = mm(inv_high[:tap_count, :], last) + mm(inv_low[:tap_count, :], last)
    skip = jnp.sum(total[...], axis=0, keepdims=True) * (2.0 / size)
    out[pl.ds(tap_count, 8), :] = jnp.broadcast_to(skip, (8, width))
    at = tap_count + 8
    for d in range(parts):
        summed = mm_nt(member[...], high[:, lanes(d, width)]) * (2.0 / size)
        sum_high, sum_low = split(summed)
        part = mm(sum_high, fwd_high[...]) + mm(sum_high, fwd_low[...]) + mm(sum_low, fwd_high[...])
        for piece in range(block // width):
            out[pl.ds(at, groups), :] = part[:, lanes(piece, width)]
            at += groups


def prepare_kernel(count, me_ref, series, gating, upstream, *refs):
    outs, (gate_held, up_held, series_sem, gate_sem, up_sem) = refs[:count], refs[count:]
    rows, channels = series.shape
    width = channels // count

    def columns(shift):
        target = lax.rem(me_ref[0] + shift, count)
        return pl.ds(pl.multiple_of(target * width, width), width)

    copies = []
    for shift, ref in enumerate(outs):
        here = columns(shift)
        copies.append(
            (
                pltpu.make_async_copy(gating.at[:, here], gate_held.at[shift], gate_sem.at[shift]),
                pltpu.make_async_copy(upstream.at[:, here], up_held.at[shift], up_sem.at[shift]),
                pltpu.make_async_copy(series.at[:, here], ref.at[:rows, :], series_sem.at[shift]),
            )
        )
    for group in copies:
        for copy in group:
            copy.start()
    for shift, ref in enumerate(outs):
        for copy in copies[shift]:
            copy.wait()
        product = up_held[shift].astype(F32) * gate_held[shift].astype(F32)
        ref[rows:, :] = product.astype(BF16)


def finish_kernel(scale, first, second, third, fourth, long_grad, taps_grad, skip_grad):
    groups, length = long_grad.shape
    tap_count, width = taps_grad.shape
    padded = first.shape[1]

    def total(at, rows):
        here = pl.ds(at, rows)
        first_pair = first[here, :].astype(F32) + second[here, :].astype(F32)
        last_pair = third[here, :].astype(F32) + fourth[here, :].astype(F32)
        return (first_pair + last_pair) * scale

    taps_grad[...] = total(0, tap_count)[:, :width]
    skip_grad[...] = total(tap_count, 8)[:1, :width]
    for piece in range(length // padded):
        long_grad[:, lanes(piece, padded)] = total(tap_count + 8 + piece * groups, groups)


def gate_kernel(order, *refs):
    count = len(order)
    me_ref, blocks, refs = refs[0], refs[1 : 1 + count], refs[1 + count :]
    gating, upstream, output, gate_grad, signal_grad = refs
    rows = gating.shape[0]
    width = blocks[0].shape[1]
    for shift, ref in zip(order, blocks):
        source = lax.rem(me_ref[0] + (count - shift), count)
        columns = pl.ds(pl.multiple_of(source * width, width), width)
        conv = ref[:rows, :].astype(F32)
        output[:, columns] = (gating[:, columns].astype(F32) * conv).astype(BF16)
        gate_grad[:, columns] = (upstream[:, columns].astype(F32) * conv).astype(BF16)
        signal_grad[:, columns] = ref[rows:, :]


def call(kernel, operands, outs, scratch, budget, micros, name, space=pltpu.VMEM):
    moved = sum(math.prod(x.shape) * x.dtype.itemsize for x in [*operands, *outs])
    return pl.pallas_call(
        kernel,
        out_shape=outs,
        in_specs=[
            SMEM if x.dtype == jnp.int32 else pl.BlockSpec(memory_space=space) for x in operands
        ],
        out_specs=[VMEM for _ in outs],
        scratch_shapes=[pltpu.VMEM(*x) if isinstance(x, tuple) else x for x in scratch],
        compiler_params=pltpu.CompilerParams(vmem_limit_bytes=budget),
        cost_estimate=pl.CostEstimate(
            flops=int(micros * 1e9), transcendentals=0, bytes_accessed=moved
        ),
        name=name,
    )(*operands)


def exchange(blocks, axis, shifts):
    count = len(blocks)
    moved = list(blocks)
    for k in shifts:
        moved[k] = lax.ppermute(blocks[k], axis, [(i, (i + k) % count) for i in range(count)])
    return moved


def columns_for(rows, me, count):
    width = rows.shape[1] // count
    return [
        lax.dynamic_slice_in_dim(rows, lax.rem(me + k, count) * width, width, 1)
        for k in range(count)
    ]


def in_order(blocks, me):
    count = len(blocks)
    order = lax.rem(me + count - jnp.arange(count), count)
    ordered = jnp.take(jnp.stack(blocks), order, axis=0)
    return jnp.transpose(ordered, (1, 0, 2)).reshape(blocks[0].shape[0], -1)


def shares(value, axis):
    value = value.astype(BF16)
    return [value] + [lax.ppermute(value, axis, [(i, i ^ flip) for i in range(4)]) for flip in (1, 2, 3)]


def local(signal, gate_input, cotangent, long_filter, short_taps, skip_gain):
    series = signal[0]
    gating = gate_input[0]
    upstream = cotangent[0]
    rows, channels = series.shape
    count = lax.axis_size("ctx")
    me = lax.axis_index("ctx")
    where = me.astype(jnp.int32).reshape(1)
    length = rows * count
    width = channels // count
    padded = -(-width // 128) * 128
    groups = long_filter.shape[0]
    tap_count = short_taps.shape[0]
    block = min(length // 4, 512)
    size = 2 * block
    parts = length // block

    def pad(x):
        return jnp.pad(x, ((0, 0), (0, padded - width))) if padded > width else x

    def trim(blocks):
        return [x[:, :width] if padded > width else x for x in blocks]

    spectrum = (size, parts * padded)
    spectrum_out = jax.ShapeDtypeStruct(spectrum, F32)
    budget = 10 * 4 * math.prod(spectrum)
    tables = [jnp.asarray(t) for t in dft_tables(block)]
    channel = np.arange(padded)[None, :]
    of_group = (channel // (width // groups) == np.arange(groups)[:, None]) & (channel < width)
    member = jnp.asarray(of_group.astype(ml_dtypes.bfloat16))
    if width % 128 == 0:
        sent = call(
            functools.partial(prepare_kernel, count),
            [where, series, gating, upstream],
            [jax.ShapeDtypeStruct((2 * rows, width), BF16)] * count,
            [((count, rows, width), BF16)] * 2 + [pltpu.SemaphoreType.DMA((count,))] * 3,
            None,
            1,
            "prepare",
            pltpu.HBM,
        )
    else:
        grad_gate = (upstream.astype(F32) * gating.astype(F32)).astype(BF16)
        sent = columns_for(jnp.concatenate([series, grad_gate]), me, count)
    out_order = [0, 1, 2, 3, 4, 5, 6, 7] if count == 8 else list(range(count))
    back_order = [0, 1, 2, 7, 3, 5, 4, 6] if count == 8 else list(range(count))
    received = [pad(x) for x in exchange(sent, "ctx", out_order[1:])]
    own_taps = pad(lax.dynamic_slice_in_dim(short_taps, me * width, width, 1))
    taps_spec, long_spec, both_spec = call(
        filters_kernel,
        [own_taps, long_filter, member, pad(skip_gain[None, :]), *tables],
        [jax.ShapeDtypeStruct((size, padded), F32), spectrum_out, spectrum_out],
        [(spectrum, BF16), (spectrum, BF16)],
        budget,
        5,
        "filters",
    )

    *outs, series_spec, grad_spec = call(
        functools.partial(conv_kernel, out_order),
        [where, *[received[k] for k in out_order], *tables, both_spec],
        [jax.ShapeDtypeStruct((2 * rows, padded), BF16)] * count + [spectrum_out] * 2,
        [((block, parts * padded), BF16), (spectrum, BF16)],
        budget,
        8,
        "conv",
    )
    outs = trim(outs)
    early, late = [1, 7], []
    returned = exchange(outs, "ctx", back_order[1:])
    *waited, grad_spec = lax.optimization_barrier([returned[k] for k in early] + [grad_spec])
    for k, value in zip(early, waited):
        returned[k] = value
    pieces = parts * (block // padded)
    (partial,) = call(
        grads_kernel,
        [grad_spec, series_spec, taps_spec, long_spec, member, *tables],
        [jax.ShapeDtypeStruct((tap_count + 8 + pieces * groups, padded), F32)],
        [(spectrum, F32), ((size, (parts + 1) * padded), BF16), ((CHUNK, padded), F32)],
        budget,
        5,
        "grads",
    )
    scale = 1.0 / math.sqrt(lax.axis_size("dp") * length)
    if lax.axis_size("dp") == 4:
        partials = shares(partial, "dp")
    else:
        partials = [lax.psum(partial, "dp")] + [jnp.zeros_like(partial)] * 3
    long_grad, taps_grad, skip_grad = call(
        functools.partial(finish_kernel, scale),
        partials,
        [
            jax.ShapeDtypeStruct((groups, length), F32),
            jax.ShapeDtypeStruct((tap_count, width), F32),
            jax.ShapeDtypeStruct((1, width), F32),
        ],
        [],
        budget,
        1,
        "finish",
    )

    full = jax.ShapeDtypeStruct((rows, channels), BF16)
    if width % 128 == 0:
        output, gate_grad, signal_grad = call(
            functools.partial(gate_kernel, back_order),
            [where, *[returned[k] for k in back_order], gating, upstream],
            [full, full, full],
            [],
            budget,
            1,
            "gate",
        )
    else:
        conv_rows, signal_grad = jnp.split(in_order(returned, me), 2)
        conv_rows = conv_rows.astype(F32)
        output = (gating.astype(F32) * conv_rows).astype(BF16)
        gate_grad = (upstream.astype(F32) * conv_rows).astype(BF16)
    return (output[None], gate_grad[None], signal_grad[None], long_grad, taps_grad, skip_grad[0])


def solution(mesh):
    return jax.shard_map(
        local,
        mesh=mesh,
        in_specs=(
            P("dp", "ctx", None),
            P("dp", "ctx", None),
            P("dp", "ctx", None),
            P("ctx", None),
            P(),
            P("ctx"),
        ),
        out_specs=(
            P("dp", "ctx", None),
            P("dp", "ctx", None),
            P("dp", "ctx", None),
            P("ctx", None),
            P(None, "ctx"),
            P("ctx"),
        ),
        check_vma=False,
    )
```

```python
import functools
import math

import jax
import jax.numpy as jnp
import ml_dtypes
import numpy as np
from jax import lax
from jax.experimental import pallas as pl
from jax.experimental.pallas import tpu as pltpu
from jax.sharding import PartitionSpec as P

BF16 = jnp.bfloat16
F32 = jnp.float32
VMEM = pl.BlockSpec(memory_space=pltpu.VMEM)
SMEM = pl.BlockSpec(memory_space=pltpu.SMEM)
CHUNK = 32


def split_table(table):
    high = table.astype(ml_dtypes.bfloat16)
    low = (table - high.astype(np.float64)).astype(ml_dtypes.bfloat16)
    return high, low


def dft_tables(block):
    size = 2 * block
    steps = ((2 * np.arange(block)[:, None] + 1) * np.arange(block)[None, :]) % (2 * size)
    angle = steps * (math.pi / size)
    table = np.concatenate([np.cos(angle), -np.sin(angle)], axis=0)
    return split_table(table) + split_table(table.T * (2.0 / size))


def mm(a, b):
    return jnp.dot(a, b, preferred_element_type=F32)


def mm_nt(a, b):
    return lax.dot_general(a, b, (((1,), (1,)), ((), ())), preferred_element_type=F32)


def mm_tn(a, b):
    return lax.dot_general(a, b, (((0,), (0,)), ((), ())), preferred_element_type=F32)


def split(x):
    high = x.astype(BF16)
    return high, (x - high.astype(F32)).astype(BF16)


def inverse(rows_high, rows_low, high, low):
    return mm(rows_high, high) + mm(rows_low, high) + mm(rows_high, low)


def parity(width):
    row = lax.broadcasted_iota(jnp.int32, (CHUNK, width), 0)
    return (1 - 2 * (row % 2)).astype(F32)


def chunks(block, body):
    def step(index, carry):
        at = pl.multiple_of(index * CHUNK, CHUNK)
        body(pl.ds(at, CHUNK), pl.ds(block + at, CHUNK))
        return carry

    lax.fori_loop(0, block // CHUNK, step, 0)


def lanes(i, width):
    return slice(i * width, (i + 1) * width)


def place_of(me_ref, step, count, rows, width, block):
    at = lax.rem(me_ref[0] + step + count, count) * rows
    row = pl.multiple_of(lax.rem(at, block), rows)
    column = pl.multiple_of(lax.div(at, block) * width, 128)
    return pl.ds(row, rows), pl.ds(column, width)


def gather_blocks(me_ref, order, blocks, which, whole, block):
    (rows, width), count = blocks[0].shape, len(blocks)
    rows //= 2
    for shift, ref in zip(order, blocks):
        row, column = place_of(me_ref, -shift, count, rows, width, block)
        part = ref[which * rows : (which + 1) * rows, :]
        whole[row, column] = part


def scatter_blocks(me_ref, whole, which, blocks, block):
    (rows, width), count = blocks[0].shape, len(blocks)
    rows //= 2
    for shift, ref in enumerate(blocks):
        ref[which * rows : (which + 1) * rows, :] = whole[place_of(me_ref, shift, count, rows, width, block)]


def filters_kernel(
    taps, long_filter, member, gain, fwd_high, fwd_low, inv_high, inv_low,
    taps_spec, long_spec, both_spec, high, low,
):
    size, block = fwd_high.shape
    tap_count, width = taps.shape
    parts = long_spec.shape[1] // width
    sign = parity(width)
    taps_spec[...] = mm(fwd_high[:, :tap_count], taps[...]) + mm(fwd_low[:, :tap_count], taps[...])
    for d in range(parts):
        part_high, part_low = split(long_filter[:, d * block : (d + 1) * block])
        spread_high = mm_tn(part_high, member[...]).astype(BF16)
        spread_low = mm_tn(part_low, member[...]).astype(BF16)
        long_spec[:, lanes(d, width)] = inverse(
            fwd_high[...], fwd_low[...], spread_high, spread_low
        )

    def product(re, im):
        long_spec[re, lanes(0, width)] = long_spec[re, lanes(0, width)] + gain[...]
        w_re, w_im = taps_spec[re, :], taps_spec[im, :]
        for d in range(parts):
            here, last = lanes(d, width), lanes(d - 1, width)
            h_re, h_im = long_spec[re, here], long_spec[im, here]
            if d:
                h_re = h_re - sign * long_spec[im, last]
                h_im = h_im + sign * long_spec[re, last]
            high[re, here], low[re, here] = split(w_re * h_re - w_im * h_im)
            high[im, here], low[im, here] = split(w_re * h_im + w_im * h_re)

    chunks(block, product)
    both = inverse(inv_high[...], inv_low[...], high[...], low[...])
    both_high, both_low = split(both)
    both_spec[...] = inverse(fwd_high[...], fwd_low[...], both_high, both_low)

    def window(re, im):
        for d in reversed(range(1, parts)):
            here, last = lanes(d, width), lanes(d - 1, width)
            both_spec[re, here] = both_spec[re, here] - sign * both_spec[im, last]
            both_spec[im, here] = both_spec[im, here] + sign * both_spec[re, last]

    chunks(block, window)


def conv_kernel(order, *refs):
    count = len(order)
    me_ref, blocks, refs = refs[0], refs[1 : 1 + count], refs[1 + count :]
    forward, inward, both_spec = refs[:3]
    outs, (series_spec, grad_spec, whole, product_spec) = refs[3 : 3 + count], refs[3 + count :]
    block = inward.shape[0]
    width = blocks[0].shape[1]
    parts = series_spec.shape[1] // width

    for which, spec in enumerate((series_spec, grad_spec)):
        backward = which == 1
        gather_blocks(me_ref, order, blocks, which, whole, block)
        spec[...] = mm(forward[...], whole[...])

        def product(re, im):
            for i in range(parts):
                sum_re = sum_im = 0.0
                for d in range(parts - i if backward else i + 1):
                    there = lanes(i + d if backward else i - d, width)
                    c_re, c_im = both_spec[re, lanes(d, width)], both_spec[im, lanes(d, width)]
                    x_re, x_im = spec[re, there], spec[im, there]
                    if backward:
                        sum_re = sum_re + (c_re * x_re + c_im * x_im)
                        sum_im = sum_im + (c_re * x_im - c_im * x_re)
                    else:
                        sum_re = sum_re + (c_re * x_re - c_im * x_im)
                        sum_im = sum_im + (c_re * x_im + c_im * x_re)
                product_spec[re, lanes(i, width)] = sum_re.astype(BF16)
                product_spec[im, lanes(i, width)] = sum_im.astype(BF16)

        chunks(block, product)
        whole[...] = mm(inward[...], product_spec[...]).astype(BF16)
        scatter_blocks(me_ref, whole, which, outs, block)


def grads_kernel(
    grad_spec, series_spec, taps_spec, long_spec, member, fwd_high, fwd_low, inv_high, inv_low,
    out, lag_spec, high, total,
):
    size, block = fwd_high.shape
    groups, width = member.shape
    parts = grad_spec.shape[1] // width
    tap_count = out.shape[0] - 8 - parts * (block // width) * groups
    sign = parity(width)

    def correlate(re, im):
        next_re = next_im = None
        for d in reversed(range(parts)):
            p_re = p_im = 0.0
            for i in range(d, parts):
                here, there = lanes(i, width), lanes(i - d, width)
                g_re, g_im = grad_spec[re, here], grad_spec[im, here]
                x_re, x_im = series_spec[re, there], series_spec[im, there]
                p_re = p_re + (g_re * x_re + g_im * x_im)
                p_im = p_im + (g_im * x_re - g_re * x_im)
            q_re, q_im = p_re, p_im
            if next_re is not None:
                q_re = q_re + sign * next_im
                q_im = q_im - sign * next_re
            high[re, lanes(d, width)] = q_re.astype(BF16)
            high[im, lanes(d, width)] = q_im.astype(BF16)
            next_re, next_im = p_re, p_im

    chunks(block, correlate)
    folded = high[:, : parts * width]
    lags = (mm(inv_high[...], folded) + mm(inv_low[...], folded)).astype(BF16)
    lag_spec[...] = mm(fwd_high[...], lags) + mm(fwd_low[...], lags)
    total[...] = jnp.zeros_like(total)

    def filtered(re, im):
        w_re, w_im = taps_spec[re, :], taps_spec[im, :]
        sum_re = sum_im = 0.0
        for d in range(parts):
            here, after = lanes(d, width), lanes(d + 1, width)
            r_re, r_im = lag_spec[re, here], lag_spec[im, here]
            if d + 1 < parts:
                r_re = r_re + sign * lag_spec[im, after]
                r_im = r_im - sign * lag_spec[re, after]
            h_re, h_im = long_spec[re, here], long_spec[im, here]
            sum_re = sum_re + (h_re * r_re + h_im * r_im)
            sum_im = sum_im + (h_re * r_im - h_im * r_re)
            v_re = w_re * r_re + w_im * r_im
            if d == 0:
                total[...] += v_re
            high[re, here] = v_re.astype(BF16)
            high[im, here] = (w_re * r_im - w_im * r_re).astype(BF16)
        last = lanes(parts, width)
        high[re, last] = sum_re.astype(BF16)
        high[im, last] = sum_im.astype(BF16)

    chunks(block, filtered)
    last = high[:, parts * width :]
    out[:tap_count, :] = mm(inv_high[:tap_count, :], last) + mm(inv_low[:tap_count, :], last)
    skip = jnp.sum(total[...], axis=0, keepdims=True) * (2.0 / size)
    out[pl.ds(tap_count, 8), :] = jnp.broadcast_to(skip, (8, width))
    at = tap_count + 8
    for d in range(parts):
        summed = mm_nt(member[...], high[:, lanes(d, width)]) * (2.0 / size)
        sum_high, sum_low = split(summed)
        part = mm(sum_high, fwd_high[...]) + mm(sum_high, fwd_low[...]) + mm(sum_low, fwd_high[...])
        for piece in range(block // width):
            out[pl.ds(at, groups), :] = part[:, lanes(piece, width)]
            at += groups


def prepare_kernel(count, me_ref, series, gating, upstream, *refs):
    outs, (gate_held, up_held, series_sem, gate_sem, up_sem) = refs[:count], refs[count:]
    rows, channels = series.shape
    width = channels // count

    def columns(shift):
        target = lax.rem(me_ref[0] + shift, count)
        return pl.ds(pl.multiple_of(target * width, width), width)

    copies = []
    for shift, ref in enumerate(outs):
        here = columns(shift)
        copies.append(
            (
                pltpu.make_async_copy(gating.at[:, here], gate_held.at[shift], gate_sem.at[shift]),
                pltpu.make_async_copy(upstream.at[:, here], up_held.at[shift], up_sem.at[shift]),
                pltpu.make_async_copy(series.at[:, here], ref.at[:rows, :], series_sem.at[shift]),
            )
        )
    for group in copies:
        for copy in group:
            copy.start()
    for shift, ref in enumerate(outs):
        for copy in copies[shift]:
            copy.wait()
        product = up_held[shift].astype(F32) * gate_held[shift].astype(F32)
        ref[rows:, :] = product.astype(BF16)


def finish_kernel(scale, first, second, third, fourth, long_grad, taps_grad, skip_grad):
    groups, length = long_grad.shape
    tap_count, width = taps_grad.shape
    padded = first.shape[1]

    def total(at, rows):
        here = pl.ds(at, rows)
        first_pair = first[here, :].astype(F32) + second[here, :].astype(F32)
        last_pair = third[here, :].astype(F32) + fourth[here, :].astype(F32)
        return (first_pair + last_pair) * scale

    taps_grad[...] = total(0, tap_count)[:, :width]
    skip_grad[...] = total(tap_count, 8)[:1, :width]
    for piece in range(length // padded):
        long_grad[:, lanes(piece, padded)] = total(tap_count + 8 + piece * groups, groups)


def gate_kernel(order, *refs):
    count = len(order)
    me_ref, blocks, refs = refs[0], refs[1 : 1 + count], refs[1 + count :]
    gating, upstream, output, gate_grad, signal_grad = refs
    rows = gating.shape[0]
    width = blocks[0].shape[1]
    for shift, ref in zip(order, blocks):
        source = lax.rem(me_ref[0] + (count - shift), count)
        columns = pl.ds(pl.multiple_of(source * width, width), width)
        conv = ref[:rows, :].astype(F32)
        output[:, columns] = (gating[:, columns].astype(F32) * conv).astype(BF16)
        gate_grad[:, columns] = (upstream[:, columns].astype(F32) * conv).astype(BF16)
        signal_grad[:, columns] = ref[rows:, :]


def call(kernel, operands, outs, scratch, budget, micros, name, space=pltpu.VMEM):
    moved = sum(math.prod(x.shape) * x.dtype.itemsize for x in [*operands, *outs])
    return pl.pallas_call(
        kernel,
        out_shape=outs,
        in_specs=[
            SMEM if x.dtype == jnp.int32 else pl.BlockSpec(memory_space=space) for x in operands
        ],
        out_specs=[VMEM for _ in outs],
        scratch_shapes=[pltpu.VMEM(*x) if isinstance(x, tuple) else x for x in scratch],
        compiler_params=pltpu.CompilerParams(vmem_limit_bytes=budget),
        cost_estimate=pl.CostEstimate(
            flops=int(micros * 1e9), transcendentals=0, bytes_accessed=moved
        ),
        name=name,
    )(*operands)


def exchange(blocks, axis, shifts):
    count = len(blocks)
    moved = list(blocks)
    for k in shifts:
        moved[k] = lax.ppermute(blocks[k], axis, [(i, (i + k) % count) for i in range(count)])
    return moved


def columns_for(rows, me, count):
    width = rows.shape[1] // count
    return [
        lax.dynamic_slice_in_dim(rows, lax.rem(me + k, count) * width, width, 1)
        for k in range(count)
    ]


def in_order(blocks, me):
    count = len(blocks)
    order = lax.rem(me + count - jnp.arange(count), count)
    ordered = jnp.take(jnp.stack(blocks), order, axis=0)
    return jnp.transpose(ordered, (1, 0, 2)).reshape(blocks[0].shape[0], -1)


def shares(value, axis):
    value = value.astype(BF16)
    return [value] + [lax.ppermute(value, axis, [(i, i ^ flip) for i in range(4)]) for flip in (1, 2, 3)]


def local(signal, gate_input, cotangent, long_filter, short_taps, skip_gain):
    series = signal[0]
    gating = gate_input[0]
    upstream = cotangent[0]
    rows, channels = series.shape
    count = lax.axis_size("ctx")
    me = lax.axis_index("ctx")
    where = me.astype(jnp.int32).reshape(1)
    length = rows * count
    width = channels // count
    padded = -(-width // 128) * 128
    groups = long_filter.shape[0]
    tap_count = short_taps.shape[0]
    block = min(length // 4, 512)
    size = 2 * block
    parts = length // block

    def pad(x):
        return jnp.pad(x, ((0, 0), (0, padded - width))) if padded > width else x

    def trim(blocks):
        return [x[:, :width] if padded > width else x for x in blocks]

    spectrum = (size, parts * padded)
    spectrum_out = jax.ShapeDtypeStruct(spectrum, F32)
    budget = 10 * 4 * math.prod(spectrum)
    tables = [jnp.asarray(t) for t in dft_tables(block)]
    forward, inward = tables[0], tables[2]
    channel = np.arange(padded)[None, :]
    of_group = (channel // (width // groups) == np.arange(groups)[:, None]) & (channel < width)
    member = jnp.asarray(of_group.astype(ml_dtypes.bfloat16))
    if width % 128 == 0:
        sent = call(
            functools.partial(prepare_kernel, count),
            [where, series, gating, upstream],
            [jax.ShapeDtypeStruct((2 * rows, width), BF16)] * count,
            [((count, rows, width), BF16)] * 2 + [pltpu.SemaphoreType.DMA((count,))] * 3,
            None,
            1,
            "prepare",
            pltpu.HBM,
        )
    else:
        grad_gate = (upstream.astype(F32) * gating.astype(F32)).astype(BF16)
        sent = columns_for(jnp.concatenate([series, grad_gate]), me, count)
    out_order = [0, 1, 2, 3, 4, 5, 6, 7] if count == 8 else list(range(count))
    back_order = [0, 1, 2, 7, 3, 5, 4, 6] if count == 8 else list(range(count))
    received = [pad(x) for x in exchange(sent, "ctx", out_order[1:])]
    own_taps = pad(lax.dynamic_slice_in_dim(short_taps, me * width, width, 1))
    taps_spec, long_spec, both_spec = call(
        filters_kernel,
        [own_taps, long_filter, member, pad(skip_gain[None, :]), *tables],
        [jax.ShapeDtypeStruct((size, padded), F32), spectrum_out, spectrum_out],
        [(spectrum, BF16), (spectrum, BF16)],
        budget,
        5,
        "filters",
    )

    *outs, series_spec, grad_spec = call(
        functools.partial(conv_kernel, out_order),
        [where, *[received[k] for k in out_order], forward, inward, both_spec],
        [jax.ShapeDtypeStruct((2 * rows, padded), BF16)] * count + [spectrum_out] * 2,
        [
            ((block, parts * padded), BF16),
            (spectrum, BF16),
        ],
        budget,
        8,
        "conv",
    )
    outs = trim(outs)
    early, late = [1, 7], []
    returned = exchange(outs, "ctx", back_order[1:])
    *waited, grad_spec = lax.optimization_barrier([returned[k] for k in early] + [grad_spec])
    for k, value in zip(early, waited):
        returned[k] = value
    pieces = parts * (block // padded)
    (partial,) = call(
        grads_kernel,
        [grad_spec, series_spec, taps_spec, long_spec, member, *tables],
        [jax.ShapeDtypeStruct((tap_count + 8 + pieces * groups, padded), F32)],
        [(spectrum, F32), ((size, (parts + 1) * padded), BF16), ((CHUNK, padded), F32)],
        budget,
        5,
        "grads",
    )
    scale = 1.0 / math.sqrt(lax.axis_size("dp") * length)
    if lax.axis_size("dp") == 4:
        partials = shares(partial, "dp")
    else:
        partials = [lax.psum(partial, "dp")] + [jnp.zeros_like(partial)] * 3
    long_grad, taps_grad, skip_grad = call(
        functools.partial(finish_kernel, scale),
        partials,
        [
            jax.ShapeDtypeStruct((groups, length), F32),
            jax.ShapeDtypeStruct((tap_count, width), F32),
            jax.ShapeDtypeStruct((1, width), F32),
        ],
        [],
        budget,
        1,
        "finish",
    )

    full = jax.ShapeDtypeStruct((rows, channels), BF16)
    if width % 128 == 0:
        output, gate_grad, signal_grad = call(
            functools.partial(gate_kernel, back_order),
            [where, *[returned[k] for k in back_order], gating, upstream],
            [full, full, full],
            [],
            budget,
            1,
            "gate",
        )
    else:
        conv_rows, signal_grad = jnp.split(in_order(returned, me), 2)
        conv_rows = conv_rows.astype(F32)
        output = (gating.astype(F32) * conv_rows).astype(BF16)
        gate_grad = (upstream.astype(F32) * conv_rows).astype(BF16)
    return (output[None], gate_grad[None], signal_grad[None], long_grad, taps_grad, skip_grad[0])


def solution(mesh):
    return jax.shard_map(
        local,
        mesh=mesh,
        in_specs=(
            P("dp", "ctx", None),
            P("dp", "ctx", None),
            P("dp", "ctx", None),
            P("ctx", None),
            P(),
            P("ctx"),
        ),
        out_specs=(
            P("dp", "ctx", None),
            P("dp", "ctx", None),
            P("dp", "ctx", None),
            P("ctx", None),
            P(None, "ctx"),
            P("ctx"),
        ),
        check_vma=False,
    )
```

```python
import functools
import math

import jax
import jax.numpy as jnp
import ml_dtypes
import numpy as np
from jax import lax
from jax.experimental import pallas as pl
from jax.experimental.pallas import tpu as pltpu
from jax.sharding import PartitionSpec as P

BF16 = jnp.bfloat16
F32 = jnp.float32
VMEM = pl.BlockSpec(memory_space=pltpu.VMEM)
SMEM = pl.BlockSpec(memory_space=pltpu.SMEM)
CHUNK = 32


def split_table(table):
    high = table.astype(ml_dtypes.bfloat16)
    low = (table - high.astype(np.float64)).astype(ml_dtypes.bfloat16)
    return high, low


def dft_tables(block):
    size = 2 * block
    steps = ((2 * np.arange(block)[:, None] + 1) * np.arange(block)[None, :]) % (2 * size)
    angle = steps * (math.pi / size)
    table = np.concatenate([np.cos(angle), -np.sin(angle)], axis=0)
    return split_table(table) + split_table(table.T * (2.0 / size))


def mm(a, b):
    return jnp.dot(a, b, preferred_element_type=F32)


def mm_nt(a, b):
    return lax.dot_general(a, b, (((1,), (1,)), ((), ())), preferred_element_type=F32)


def mm_tn(a, b):
    return lax.dot_general(a, b, (((0,), (0,)), ((), ())), preferred_element_type=F32)


def split(x):
    high = x.astype(BF16)
    return high, (x - high.astype(F32)).astype(BF16)


def inverse(rows_high, rows_low, high, low):
    return mm(rows_high, high) + mm(rows_low, high) + mm(rows_high, low)


def parity(width):
    row = lax.broadcasted_iota(jnp.int32, (CHUNK, width), 0)
    return (1 - 2 * (row % 2)).astype(F32)


def chunks(block, body):
    def step(index, carry):
        at = pl.multiple_of(index * CHUNK, CHUNK)
        body(pl.ds(at, CHUNK), pl.ds(block + at, CHUNK))
        return carry

    lax.fori_loop(0, block // CHUNK, step, 0)


def lanes(i, width):
    return slice(i * width, (i + 1) * width)


def place_of(me_ref, step, count, rows, width, block):
    at = lax.rem(me_ref[0] + step + count, count) * rows
    row = pl.multiple_of(lax.rem(at, block), rows)
    column = pl.multiple_of(lax.div(at, block) * width, 128)
    return pl.ds(row, rows), pl.ds(column, width)


def gather_blocks(me_ref, order, blocks, which, whole, block):
    (rows, width), count = blocks[0].shape, len(blocks)
    rows //= 2
    for shift, ref in zip(order, blocks):
        row, column = place_of(me_ref, -shift, count, rows, width, block)
        part = ref[which * rows : (which + 1) * rows, :]
        whole[row, column] = part


def scatter_blocks(me_ref, whole, which, blocks, block):
    (rows, width), count = blocks[0].shape, len(blocks)
    rows //= 2
    for shift, ref in enumerate(blocks):
        ref[which * rows : (which + 1) * rows, :] = whole[place_of(me_ref, shift, count, rows, width, block)]


def filters_kernel(
    taps, long_filter, member, gain, fwd_high, fwd_low, inv_high, inv_low,
    taps_spec, long_spec, both_spec, high, low,
):
    size, block = fwd_high.shape
    tap_count, width = taps.shape
    parts = long_spec.shape[1] // width
    sign = parity(width)
    taps_spec[...] = mm(fwd_high[:, :tap_count], taps[...]) + mm(fwd_low[:, :tap_count], taps[...])
    for d in range(parts):
        part_high, part_low = split(long_filter[:, d * block : (d + 1) * block])
        spread_high = mm_tn(part_high, member[...]).astype(BF16)
        spread_low = mm_tn(part_low, member[...]).astype(BF16)
        long_spec[:, lanes(d, width)] = inverse(
            fwd_high[...], fwd_low[...], spread_high, spread_low
        )

    def product(re, im):
        long_spec[re, lanes(0, width)] = long_spec[re, lanes(0, width)] + gain[...]
        w_re, w_im = taps_spec[re, :], taps_spec[im, :]
        for d in range(parts):
            here, last = lanes(d, width), lanes(d - 1, width)
            h_re, h_im = long_spec[re, here], long_spec[im, here]
            if d:
                h_re = h_re - sign * long_spec[im, last]
                h_im = h_im + sign * long_spec[re, last]
            high[re, here], low[re, here] = split(w_re * h_re - w_im * h_im)
            high[im, here], low[im, here] = split(w_re * h_im + w_im * h_re)

    chunks(block, product)
    both = inverse(inv_high[...], inv_low[...], high[...], low[...])
    both_high, both_low = split(both)
    both_spec[...] = inverse(fwd_high[...], fwd_low[...], both_high, both_low)

    def window(re, im):
        for d in reversed(range(1, parts)):
            here, last = lanes(d, width), lanes(d - 1, width)
            both_spec[re, here] = both_spec[re, here] - sign * both_spec[im, last]
            both_spec[im, here] = both_spec[im, here] + sign * both_spec[re, last]

    chunks(block, window)


def conv_kernel(order, *refs):
    count = len(order)
    me_ref, blocks, refs = refs[0], refs[1 : 1 + count], refs[1 + count :]
    forward, inward, both_spec = refs[:3]
    outs, (series_spec, grad_spec, whole, product_spec) = refs[3 : 3 + count], refs[3 + count :]
    block = inward.shape[0]
    width = blocks[0].shape[1]
    parts = series_spec.shape[1] // width

    for which, spec in enumerate((series_spec, grad_spec)):
        backward = which == 1
        gather_blocks(me_ref, order, blocks, which, whole, block)
        spec[...] = mm(forward[...], whole[...])

        def product(re, im):
            for i in range(parts):
                sum_re = sum_im = 0.0
                for d in range(parts - i if backward else i + 1):
                    there = lanes(i + d if backward else i - d, width)
                    c_re, c_im = both_spec[re, lanes(d, width)], both_spec[im, lanes(d, width)]
                    x_re, x_im = spec[re, there], spec[im, there]
                    if backward:
                        sum_re = sum_re + (c_re * x_re + c_im * x_im)
                        sum_im = sum_im + (c_re * x_im - c_im * x_re)
                    else:
                        sum_re = sum_re + (c_re * x_re - c_im * x_im)
                        sum_im = sum_im + (c_re * x_im + c_im * x_re)
                product_spec[re, lanes(i, width)] = sum_re.astype(BF16)
                product_spec[im, lanes(i, width)] = sum_im.astype(BF16)

        chunks(block, product)
        whole[...] = mm(inward[...], product_spec[...]).astype(BF16)
        scatter_blocks(me_ref, whole, which, outs, block)


def grads_kernel(
    grad_spec, series_spec, taps_spec, long_spec, member, fwd_high, fwd_low, inv_high, inv_low,
    out, lag_spec, high, total,
):
    size, block = fwd_high.shape
    groups, width = member.shape
    parts = grad_spec.shape[1] // width
    tap_count = out.shape[0] - 8 - parts * (block // width) * groups
    sign = parity(width)

    def correlate(re, im):
        next_re = next_im = None
        for d in reversed(range(parts)):
            p_re = p_im = 0.0
            for i in range(d, parts):
                here, there = lanes(i, width), lanes(i - d, width)
                g_re, g_im = grad_spec[re, here], grad_spec[im, here]
                x_re, x_im = series_spec[re, there], series_spec[im, there]
                p_re = p_re + (g_re * x_re + g_im * x_im)
                p_im = p_im + (g_im * x_re - g_re * x_im)
            q_re, q_im = p_re, p_im
            if next_re is not None:
                q_re = q_re + sign * next_im
                q_im = q_im - sign * next_re
            high[re, lanes(d, width)] = q_re.astype(BF16)
            high[im, lanes(d, width)] = q_im.astype(BF16)
            next_re, next_im = p_re, p_im

    chunks(block, correlate)
    folded = high[:, : parts * width]
    lags = mm(inv_high[...], folded).astype(BF16)
    lag_spec[...] = mm(fwd_high[...], lags) + mm(fwd_low[...], lags)
    total[...] = jnp.zeros_like(total)

    def filtered(re, im):
        w_re, w_im = taps_spec[re, :], taps_spec[im, :]
        sum_re = sum_im = 0.0
        for d in range(parts):
            here, after = lanes(d, width), lanes(d + 1, width)
            r_re, r_im = lag_spec[re, here], lag_spec[im, here]
            if d + 1 < parts:
                r_re = r_re + sign * lag_spec[im, after]
                r_im = r_im - sign * lag_spec[re, after]
            h_re, h_im = long_spec[re, here], long_spec[im, here]
            sum_re = sum_re + (h_re * r_re + h_im * r_im)
            sum_im = sum_im + (h_re * r_im - h_im * r_re)
            v_re = w_re * r_re + w_im * r_im
            if d == 0:
                total[...] += v_re
            high[re, here] = v_re.astype(BF16)
            high[im, here] = (w_re * r_im - w_im * r_re).astype(BF16)
        last = lanes(parts, width)
        high[re, last] = sum_re.astype(BF16)
        high[im, last] = sum_im.astype(BF16)

    chunks(block, filtered)
    last = high[:, parts * width :]
    out[:tap_count, :] = mm(inv_high[:tap_count, :], last) + mm(inv_low[:tap_count, :], last)
    skip = jnp.sum(total[...], axis=0, keepdims=True) * (2.0 / size)
    out[pl.ds(tap_count, 8), :] = jnp.broadcast_to(skip, (8, width))
    at = tap_count + 8
    for d in range(parts):
        summed = mm_nt(member[...], high[:, lanes(d, width)]) * (2.0 / size)
        sum_high, sum_low = split(summed)
        part = mm(sum_high, fwd_high[...]) + mm(sum_high, fwd_low[...]) + mm(sum_low, fwd_high[...])
        for piece in range(block // width):
            out[pl.ds(at, groups), :] = part[:, lanes(piece, width)]
            at += groups


def prepare_kernel(count, me_ref, series, gating, upstream, *refs):
    outs, (gate_held, up_held, series_sem, gate_sem, up_sem) = refs[:count], refs[count:]
    rows, channels = series.shape
    width = channels // count

    def columns(shift):
        target = lax.rem(me_ref[0] + shift, count)
        return pl.ds(pl.multiple_of(target * width, width), width)

    copies = []
    for shift, ref in enumerate(outs):
        here = columns(shift)
        copies.append(
            (
                pltpu.make_async_copy(gating.at[:, here], gate_held.at[shift], gate_sem.at[shift]),
                pltpu.make_async_copy(upstream.at[:, here], up_held.at[shift], up_sem.at[shift]),
                pltpu.make_async_copy(series.at[:, here], ref.at[:rows, :], series_sem.at[shift]),
            )
        )
    for group in copies:
        for copy in group:
            copy.start()
    for shift, ref in enumerate(outs):
        for copy in copies[shift]:
            copy.wait()
        product = up_held[shift].astype(F32) * gate_held[shift].astype(F32)
        ref[rows:, :] = product.astype(BF16)


def finish_kernel(scale, first, second, third, fourth, long_grad, taps_grad, skip_grad):
    groups, length = long_grad.shape
    tap_count, width = taps_grad.shape
    padded = first.shape[1]

    def total(at, rows):
        here = pl.ds(at, rows)
        first_pair = first[here, :].astype(F32) + second[here, :].astype(F32)
        last_pair = third[here, :].astype(F32) + fourth[here, :].astype(F32)
        return (first_pair + last_pair) * scale

    taps_grad[...] = total(0, tap_count)[:, :width]
    skip_grad[...] = total(tap_count, 8)[:1, :width]
    for piece in range(length // padded):
        long_grad[:, lanes(piece, padded)] = total(tap_count + 8 + piece * groups, groups)


def gate_kernel(order, *refs):
    count = len(order)
    me_ref, blocks, refs = refs[0], refs[1 : 1 + count], refs[1 + count :]
    gating, upstream, output, gate_grad, signal_grad = refs
    rows = gating.shape[0]
    width = blocks[0].shape[1]
    for shift, ref in zip(order, blocks):
        source = lax.rem(me_ref[0] + (count - shift), count)
        columns = pl.ds(pl.multiple_of(source * width, width), width)
        conv = ref[:rows, :].astype(F32)
        output[:, columns] = (gating[:, columns].astype(F32) * conv).astype(BF16)
        gate_grad[:, columns] = (upstream[:, columns].astype(F32) * conv).astype(BF16)
        signal_grad[:, columns] = ref[rows:, :]


def call(kernel, operands, outs, scratch, budget, micros, name, space=pltpu.VMEM):
    moved = sum(math.prod(x.shape) * x.dtype.itemsize for x in [*operands, *outs])
    return pl.pallas_call(
        kernel,
        out_shape=outs,
        in_specs=[
            SMEM if x.dtype == jnp.int32 else pl.BlockSpec(memory_space=space) for x in operands
        ],
        out_specs=[VMEM for _ in outs],
        scratch_shapes=[pltpu.VMEM(*x) if isinstance(x, tuple) else x for x in scratch],
        compiler_params=pltpu.CompilerParams(vmem_limit_bytes=budget),
        cost_estimate=pl.CostEstimate(
            flops=int(micros * 1e9), transcendentals=0, bytes_accessed=moved
        ),
        name=name,
    )(*operands)


def exchange(blocks, axis, shifts):
    count = len(blocks)
    moved = list(blocks)
    for k in shifts:
        moved[k] = lax.ppermute(blocks[k], axis, [(i, (i + k) % count) for i in range(count)])
    return moved


def columns_for(rows, me, count):
    width = rows.shape[1] // count
    return [
        lax.dynamic_slice_in_dim(rows, lax.rem(me + k, count) * width, width, 1)
        for k in range(count)
    ]


def in_order(blocks, me):
    count = len(blocks)
    order = lax.rem(me + count - jnp.arange(count), count)
    ordered = jnp.take(jnp.stack(blocks), order, axis=0)
    return jnp.transpose(ordered, (1, 0, 2)).reshape(blocks[0].shape[0], -1)


def shares(value, axis):
    value = value.astype(BF16)
    return [value] + [lax.ppermute(value, axis, [(i, i ^ flip) for i in range(4)]) for flip in (1, 2, 3)]


def local(signal, gate_input, cotangent, long_filter, short_taps, skip_gain):
    series = signal[0]
    gating = gate_input[0]
    upstream = cotangent[0]
    rows, channels = series.shape
    count = lax.axis_size("ctx")
    me = lax.axis_index("ctx")
    where = me.astype(jnp.int32).reshape(1)
    length = rows * count
    width = channels // count
    padded = -(-width // 128) * 128
    groups = long_filter.shape[0]
    tap_count = short_taps.shape[0]
    block = min(length // 4, 512)
    size = 2 * block
    parts = length // block

    def pad(x):
        return jnp.pad(x, ((0, 0), (0, padded - width))) if padded > width else x

    def trim(blocks):
        return [x[:, :width] if padded > width else x for x in blocks]

    spectrum = (size, parts * padded)
    spectrum_out = jax.ShapeDtypeStruct(spectrum, F32)
    budget = 10 * 4 * math.prod(spectrum)
    tables = [jnp.asarray(t) for t in dft_tables(block)]
    forward, inward = tables[0], tables[2]
    channel = np.arange(padded)[None, :]
    of_group = (channel // (width // groups) == np.arange(groups)[:, None]) & (channel < width)
    member = jnp.asarray(of_group.astype(ml_dtypes.bfloat16))
    if width % 128 == 0:
        sent = call(
            functools.partial(prepare_kernel, count),
            [where, series, gating, upstream],
            [jax.ShapeDtypeStruct((2 * rows, width), BF16)] * count,
            [((count, rows, width), BF16)] * 2 + [pltpu.SemaphoreType.DMA((count,))] * 3,
            None,
            1,
            "prepare",
            pltpu.HBM,
        )
    else:
        grad_gate = (upstream.astype(F32) * gating.astype(F32)).astype(BF16)
        sent = columns_for(jnp.concatenate([series, grad_gate]), me, count)
    out_order = [0, 1, 2, 3, 4, 5, 6, 7] if count == 8 else list(range(count))
    back_order = [0, 1, 2, 7, 3, 5, 4, 6] if count == 8 else list(range(count))
    received = [pad(x) for x in exchange(sent, "ctx", out_order[1:])]
    own_taps = pad(lax.dynamic_slice_in_dim(short_taps, me * width, width, 1))
    taps_spec, long_spec, both_spec = call(
        filters_kernel,
        [own_taps, long_filter, member, pad(skip_gain[None, :]), *tables],
        [jax.ShapeDtypeStruct((size, padded), F32), spectrum_out, spectrum_out],
        [(spectrum, BF16), (spectrum, BF16)],
        budget,
        5,
        "filters",
    )

    *outs, series_spec, grad_spec = call(
        functools.partial(conv_kernel, out_order),
        [where, *[received[k] for k in out_order], forward, inward, both_spec],
        [jax.ShapeDtypeStruct((2 * rows, padded), BF16)] * count + [spectrum_out] * 2,
        [
            ((block, parts * padded), BF16),
            (spectrum, BF16),
        ],
        budget,
        8,
        "conv",
    )
    outs = trim(outs)
    early, late = [1, 7], []
    returned = exchange(outs, "ctx", back_order[1:])
    *waited, grad_spec = lax.optimization_barrier([returned[k] for k in early] + [grad_spec])
    for k, value in zip(early, waited):
        returned[k] = value
    pieces = parts * (block // padded)
    (partial,) = call(
        grads_kernel,
        [grad_spec, series_spec, taps_spec, long_spec, member, *tables],
        [jax.ShapeDtypeStruct((tap_count + 8 + pieces * groups, padded), F32)],
        [(spectrum, F32), ((size, (parts + 1) * padded), BF16), ((CHUNK, padded), F32)],
        budget,
        5,
        "grads",
    )
    scale = 1.0 / math.sqrt(lax.axis_size("dp") * length)
    if lax.axis_size("dp") == 4:
        partials = shares(partial, "dp")
    else:
        partials = [lax.psum(partial, "dp")] + [jnp.zeros_like(partial)] * 3
    long_grad, taps_grad, skip_grad = call(
        functools.partial(finish_kernel, scale),
        partials,
        [
            jax.ShapeDtypeStruct((groups, length), F32),
            jax.ShapeDtypeStruct((tap_count, width), F32),
            jax.ShapeDtypeStruct((1, width), F32),
        ],
        [],
        budget,
        1,
        "finish",
    )

    full = jax.ShapeDtypeStruct((rows, channels), BF16)
    if width % 128 == 0:
        output, gate_grad, signal_grad = call(
            functools.partial(gate_kernel, back_order),
            [where, *[returned[k] for k in back_order], gating, upstream],
            [full, full, full],
            [],
            budget,
            1,
            "gate",
        )
    else:
        conv_rows, signal_grad = jnp.split(in_order(returned, me), 2)
        conv_rows = conv_rows.astype(F32)
        output = (gating.astype(F32) * conv_rows).astype(BF16)
        gate_grad = (upstream.astype(F32) * conv_rows).astype(BF16)
    return (output[None], gate_grad[None], signal_grad[None], long_grad, taps_grad, skip_grad[0])


def solution(mesh):
    return jax.shard_map(
        local,
        mesh=mesh,
        in_specs=(
            P("dp", "ctx", None),
            P("dp", "ctx", None),
            P("dp", "ctx", None),
            P("ctx", None),
            P(),
            P("ctx"),
        ),
        out_specs=(
            P("dp", "ctx", None),
            P("dp", "ctx", None),
            P("dp", "ctx", None),
            P("ctx", None),
            P(None, "ctx"),
            P("ctx"),
        ),
        check_vma=False,
    )
```
